128 devices in a mesh: dom: 128 (over x, z, y, core).
Axes of the slice: x: 4, y: 4, z: 4, core: 2. Of those that a mesh axis runs over, the one named last changes fastest.
Arguments:
- features: bfloat16 [65536, 512], P('dom'), may hold values from -6 to 6
- weight_self: bfloat16 [512, 512], replicated, may hold values from -0.25 to 0.25
- weight_neigh: bfloat16 [512, 512], replicated, may hold values from -3 to 3
- local_weight: bfloat16 [65536, 512], P('dom'), may hold values from 0.049804688 to 1
- tile_cols: int32 [512, 4], P('dom'), may hold values from 0 to 3
- cut_weight: bfloat16 [65536, 512], P('dom'), may hold values from 0.049804688 to 1
- send_rows: int32 [16384, 4], P('dom'), may hold values from 0 to 255
- send_count: int32 [128, 128], P(None, 'dom'), may hold values from 0 to 4, as said below
- hub_rows: int32 [2048], P('dom'), may hold values from 0 to 255
- hub_edges: int32 [65536, 8], P('dom'), may hold values from 0 to 2047
- hub_weight: bfloat16 [65536, 8], P('dom'), may hold values from 1 to 16
- row_counts: int32 [128], P('dom'), may hold values from 256 to 512, as said below
- cotangent: bfloat16 [65536, 512], P('dom'), may hold values from -6 to 6
Outputs:
- activated: bfloat16 [65536, 512], P('dom')
- feature_grad: bfloat16 [65536, 512], P('dom')
- grad_self: float32 [512, 512], replicated
- grad_neigh: float32 [512, 512], replicated
The draws below stay inside these ranges and needn't reach their ends.
Inputs may be any that keep to these rules, and one draw needn't show every extreme that they name: `send_count`: the used slots from one partition to another are the first ones; some partition receives all 4 slots from every partition. `row_counts`: the live rows of a partition are its leading rows; some partition has all rows live. `hub_rows`: hub h is owned by partition h // 16; its row there is live. `send_rows`: every sent row is live.
All inputs are finite; a program needn't handle non-finite values.
Results may differ from the reference program's by a relative error of at most 0.0056.
Values may be sent and summed in bfloat16 or wider, within the bound.
No kernel may reach another device: no remote copies, remote signals or barrier semaphores. Data moves between devices by JAX's collectives and lax.ppermute only.
A program may use at most 64 MiB of HBM per device.

```python
import math
import jax
import jax.numpy as jnp
import numpy as np
from jax import lax

F = 512
TILE = 128
V_DEV = 512
TPR = 4
CUT_B = 4
HUB_DEV = 16
HE = 8
V = 65536
H = 2048
N_DOM = 128


def draw_send_count(key, part):
    first_key = jax.random.fold_in(key, 11)
    second_key = jax.random.fold_in(key, 12)
    counts = jax.random.randint(first_key, (N_DOM, N_DOM), 0, CUT_B + 1)
    chosen_col = jax.random.randint(second_key, (), 0, N_DOM)
    column = jnp.arange(N_DOM, dtype=jnp.int32)[None, :] == chosen_col
    return jnp.where(column, CUT_B, counts).astype(jnp.int32)


def draw_row_counts(key, part):
    first_key = jax.random.fold_in(key, 21)
    second_key = jax.random.fold_in(key, 22)
    counts = jax.random.randint(first_key, (N_DOM,), V_DEV // 2, V_DEV + 1)
    chosen_part = jax.random.randint(second_key, (), 0, N_DOM)
    return jnp.where(jnp.arange(N_DOM, dtype=jnp.int32) == chosen_part, V_DEV, counts).astype(jnp.int32)


def with_ends(array, rng, least, high):
    longest = array.shape.index(max(array.shape))
    spots = []
    for shift in (0, 1):
        where = [jax.random.randint(jax.random.fold_in(rng, axis), (), 0, length) for axis, length in enumerate(array.shape)]
        where[longest] = (where[longest] + shift) % array.shape[longest]
        spots.append(tuple(where))
    return array.at[spots[0]].set(least).at[spots[1]].set(high)


def block_levels(own_key, dims, pieces, least, high):
    factor_of = 1.0
    for axis_at, shards_of in pieces:
        heights = jax.random.uniform(jax.random.fold_in(jax.random.fold_in(own_key, 6), axis_at), (shards_of,), jnp.float32, least / len(pieces), high / len(pieces))
        factor_of = factor_of * jnp.repeat(jnp.exp(heights), dims[axis_at] // shards_of).reshape((-1,) + (1,) * (len(dims) - 1 - axis_at))
    return factor_of


def rank_table(number_of, slope):
    loads = [(1 << 20) // math.isqrt(grade ** slope) + 1 for grade in range(1, number_of + 1)]
    spread = 1 + sum(loads) // (1 << 30)
    return np.cumsum(np.array([max(1, weight // spread) for weight in loads]))


def skewed_ids(own_key, extent, number_of, lean):
    table = rank_table(number_of, lean)
    ticket = jax.random.randint(jax.random.fold_in(own_key, 1), extent, 0, int(table[number_of - 1]))
    grade = jnp.searchsorted(jnp.asarray(table, jnp.int32), ticket, side="right")
    return jax.random.permutation(jax.random.fold_in(own_key, 2), number_of)[grade].astype(jnp.int32)


def normal_values(rng, shape, width, most, pieces=(), kind=jnp.bfloat16):
    values = jax.random.normal(rng, shape, jnp.float32) * width
    if len(pieces) > 0:
        values = block_levels(rng, shape, pieces, -0.22, 0.18) * values
    return jnp.clip(values, min=-most, max=most).astype(kind)


def setup_inputs(seed: int = 0) -> dict:
    seeds = jax.random.split(jax.random.key(seed), 14)
    return {
        "features": normal_values(seeds[0], (V, F), 1.0, 6.0, ((0, 128),)),
        "weight_self": normal_values(seeds[1], (F, F), F ** -0.5, 0.25),
        "weight_neigh": normal_values(seeds[2], (F, F), (max(F // 128, 1)) ** -0.5, 3.0),
        "local_weight": jnp.clip(jnp.exp(math.log(1.0) - 2.9996462 * jax.random.uniform(seeds[3], (V, TPR * TILE), jnp.float32) ** block_levels(seeds[3], (V, TPR * TILE), ((0, 128),), -0.2, 0.2)), 0.049804688, 1.0).astype(jnp.bfloat16),
        "tile_cols": with_ends(jax.random.randint(seeds[4], (V // TILE, TPR), 0, V_DEV // TILE), jax.random.fold_in(seeds[4], 1), 0, (V_DEV // TILE) - 1).astype(jnp.int32),
        "cut_weight": jnp.clip(jnp.exp(math.log(1.0) - 2.9996462 * jax.random.uniform(seeds[5], (V, N_DOM * CUT_B), jnp.float32) ** block_levels(seeds[5], (V, N_DOM * CUT_B), ((0, 128),), -0.2, 0.2)), 0.049804688, 1.0).astype(jnp.bfloat16),
        "send_rows": with_ends(jax.random.randint(seeds[6], (N_DOM * N_DOM, CUT_B), 0, V_DEV // 2), jax.random.fold_in(seeds[6], 1), 0, (V_DEV // 2) - 1).astype(jnp.int32),
        "send_count": draw_send_count(jax.random.fold_in(seeds[13], 71), 0),
        "hub_rows": with_ends(jax.random.randint(seeds[8], (H,), 0, V_DEV // 2), jax.random.fold_in(seeds[8], 1), 0, (V_DEV // 2) - 1).astype(jnp.int32),
        "hub_edges": with_ends(skewed_ids(seeds[9], (V, HE), H, 1), jax.random.fold_in(seeds[9], 3), 0, H - 1).astype(jnp.int32),
        "hub_weight": jnp.clip(jnp.exp(math.log(16.0) - 2.7725887 * jax.random.uniform(seeds[10], (V, HE), jnp.float32) ** block_levels(seeds[10], (V, HE), ((0, 128),), -0.2, 0.2)), 1.0, 16.0).astype(jnp.bfloat16),
        "row_counts": draw_row_counts(jax.random.fold_in(seeds[13], 71), 0),
        "cotangent": normal_values(seeds[12], (V, F), 1.0, 6.0, ((0, 128),)),
    }


def dedup_weights(edge_ids, eweight):
    wide = eweight.astype(jnp.float32)
    same = edge_ids[:, :, None] == edge_ids[:, None, :]
    combined = jnp.sum(jnp.where(same, wide[:, None, :], jnp.zeros((), jnp.float32)), axis=2)
    order = jnp.arange(HE, dtype=jnp.int32)
    earlier = jnp.any(same & (order[None, None, :] < order[None, :, None]), axis=2)
    return jnp.where(earlier, jnp.zeros((), jnp.float32), combined).astype(jnp.bfloat16)


def reference(features, weight_self, weight_neigh, local_weight, tile_cols, cut_weight, send_rows, send_count, hub_rows, hub_edges, hub_weight, row_counts, cotangent):
    part_count = N_DOM
    blocks = V_DEV // TILE
    positions = jnp.arange(V_DEV, dtype=jnp.int32)
    row_live = positions[None, :] < row_counts[:, None]
    masked = jnp.where(row_live[:, :, None], features.reshape(part_count, V_DEV, F), jnp.zeros((), jnp.bfloat16))
    owners = jnp.arange(part_count, dtype=jnp.int32)
    hub_table = masked[owners[:, None], hub_rows.reshape(part_count, HUB_DEV)].reshape(part_count * HUB_DEV, F)
    routes = send_rows.reshape(part_count, part_count, CUT_B)
    outgoing = masked[owners[:, None, None], routes]
    incoming = jnp.swapaxes(outgoing, 0, 1).reshape(part_count, part_count * CUT_B, F)
    slot_live = jnp.arange(CUT_B, dtype=jnp.int32)[None, None, :] < send_count[:, :, None]
    slot_live = jnp.swapaxes(slot_live, 0, 1).reshape(part_count, part_count * CUT_B)

    def device_pass(totals, device_item):
        sum_self, sum_neigh, hub_grad = totals
        feat_rows, lweight, col_ids, cweight, slot_mask, received, edge_ids, eweight, live_rows, cot_rows = device_item
        live_mask = live_rows.astype(jnp.float32)
        tile_vals = lweight.reshape(blocks, TILE, TPR, TILE).astype(jnp.float32)
        picked = feat_rows.reshape(blocks, TILE, F)[col_ids].astype(jnp.float32)
        local_sum = jnp.einsum("rits,rtsf->rif", tile_vals, picked).reshape(V_DEV, F)
        live_pick = live_mask.reshape(blocks, TILE)[col_ids]
        local_deg = jnp.einsum("rits,rts->ri", tile_vals, live_pick).reshape(V_DEV)
        cut_masked = cweight * slot_mask[None, :].astype(jnp.bfloat16)
        cut_sum = jnp.dot(cut_masked, received, preferred_element_type=jnp.float32)
        cut_deg = jnp.sum(cut_masked.astype(jnp.float32), axis=1)
        eff_weight = dedup_weights(edge_ids, eweight).astype(jnp.float32)
        hub_sum = jnp.zeros((V_DEV, F), jnp.float32)
        for column in range(HE):
            hub_sum = hub_sum + eff_weight[:, column:column + 1] * hub_table[edge_ids[:, column]].astype(jnp.float32)
        hub_deg = jnp.sum(eweight.astype(jnp.float32), axis=1)
        degree = local_deg + cut_deg + hub_deg
        mean_agg = ((local_sum + cut_sum + hub_sum) / degree[:, None]).astype(jnp.bfloat16)
        pre_act = jnp.dot(feat_rows, weight_self, preferred_element_type=jnp.float32) + jnp.dot(mean_agg, weight_neigh, preferred_element_type=jnp.float32)
        gate_sig = jax.nn.sigmoid(pre_act)
        activated = (pre_act * gate_sig * live_mask[:, None]).astype(jnp.bfloat16)
        grad_pre = (cot_rows.astype(jnp.float32) * gate_sig * (1.0 + pre_act * (1.0 - gate_sig)) * live_mask[:, None]).astype(jnp.bfloat16)
        sum_self = sum_self + jnp.dot(feat_rows.T, grad_pre, preferred_element_type=jnp.float32)
        sum_neigh = sum_neigh + jnp.dot(mean_agg.T, grad_pre, preferred_element_type=jnp.float32)
        grad_agg = jnp.dot(grad_pre, weight_neigh.T, preferred_element_type=jnp.float32)
        grad_mean = (grad_agg / degree[:, None]).astype(jnp.bfloat16)
        grad_rows = jnp.dot(grad_pre, weight_self.T, preferred_element_type=jnp.float32)
        contrib = jnp.einsum("rits,rif->rtsf", tile_vals, grad_mean.reshape(blocks, TILE, F).astype(jnp.float32))
        grad_blocks = jnp.zeros((blocks, TILE, F), jnp.float32).at[col_ids.reshape(-1)].add(contrib.reshape(blocks * TPR, TILE, F))
        grad_rows = grad_rows + grad_blocks.reshape(V_DEV, F)
        cut_back = jnp.dot(cut_masked.T, grad_mean, preferred_element_type=jnp.float32)
        grad_mean_f = grad_mean.astype(jnp.float32)
        for column in range(HE):
            hub_grad = hub_grad.at[edge_ids[:, column]].add(eff_weight[:, column:column + 1] * grad_mean_f)
        return (sum_self, sum_neigh, hub_grad), (activated, grad_rows, cut_back)

    start = (jnp.zeros((F, F), jnp.float32), jnp.zeros((F, F), jnp.float32), jnp.zeros((part_count * HUB_DEV, F), jnp.float32))
    items = (masked,
             local_weight.reshape(part_count, V_DEV, TPR * TILE),
             tile_cols.reshape(part_count, blocks, TPR),
             cut_weight.reshape(part_count, V_DEV, part_count * CUT_B),
             slot_live, incoming,
             hub_edges.reshape(part_count, V_DEV, HE),
             hub_weight.reshape(part_count, V_DEV, HE),
             row_live,
             cotangent.reshape(part_count, V_DEV, F))
    (sum_self, sum_neigh, hub_grad), (act_all, part_all, back_all) = lax.scan(device_pass, start, items)
    back = jnp.swapaxes(back_all.reshape(part_count, part_count, CUT_B, F), 0, 1)
    grad_all = part_all.at[owners[:, None, None], routes].add(back)
    grad_all = grad_all.at[owners[:, None], hub_rows.reshape(part_count, HUB_DEV)].add(hub_grad.reshape(part_count, HUB_DEV, F))
    feature_grad = (grad_all * row_live[:, :, None].astype(jnp.float32)).astype(jnp.bfloat16).reshape(part_count * V_DEV, F)
    return act_all.reshape(part_count * V_DEV, F), feature_grad, sum_self, sum_neigh
```

```python
import functools

import jax
import jax.numpy as jnp
from jax import lax
from jax.experimental import pallas as pl
from jax.experimental.pallas import tpu as pltpu
from jax.sharding import Mesh
from jax.sharding import PartitionSpec as P

TILE = 128
TPR = 4
DOM = ("dom_0", "dom_1", "dom_2", "dom_3")
CHIPS = DOM[:3]
CORE = "dom_3"
BF = jnp.bfloat16
F32 = jnp.float32
REACH = 256


VM = pl.BlockSpec(memory_space=pltpu.VMEM)
SM = pl.BlockSpec(memory_space=pltpu.SMEM)


def call(body, outs, specs, flops, *args):
    size = sum(a.size * a.dtype.itemsize for a in args)
    size += sum(o.size * o.dtype.itemsize for o in outs)
    return pl.pallas_call(
        body,
        out_shape=tuple(outs),
        in_specs=list(specs),
        out_specs=tuple([VM] * len(outs)),
        name=body.__name__,
        cost_estimate=pl.CostEstimate(flops=flops, bytes_accessed=size, transcendentals=0),
    )(*args)


def mm(a, b):
    return jnp.dot(a, b, preferred_element_type=F32)


def mm_nt(a, b):
    return lax.dot_general(a, b, (((1,), (1,)), ((), ())), preferred_element_type=F32)


def mm_tn(a, b):
    return lax.dot_general(a, b, (((0,), (0,)), ((), ())), preferred_element_type=F32)


def pair(x):
    return lax.ppermute(x, CORE, [(0, 1), (1, 0)])


def over_chips(x):
    return lax.all_to_all(x, CHIPS, 0, 0, tiled=True)


def hot(ids, shape, dim):
    return jnp.where(ids == lax.broadcasted_iota(jnp.int32, shape, dim), 1.0, 0.0).astype(BF)


def hub_send(ids, feats, out):
    peers, width, feat = out.shape
    slab = mm(hot(ids[...], (width, REACH), 1), feats[:REACH, :]).astype(BF)
    out[...] = jnp.broadcast_to(slab[None], out.shape)


def cut_send(ids, feats, other, out):
    slots = ids.shape[0]
    near = mm(hot(ids[...], (slots, REACH), 1), feats[:REACH, :])
    far = mm(hot(ids[...] - REACH, (slots, REACH), 1), other[:REACH, :])
    out[...] = (near + far).astype(BF).reshape(out.shape)


def ahead(
    cols,
    count,
    core,
    feats,
    lweight,
    cweight,
    slots,
    ids,
    idw,
    hubw,
    wself,
    other,
    local_sum,
    self_term,
    degree,
    cut_mask,
    dense,
    flip_own,
    flip_out,
    cut_own,
    cut_out,
    feat_own,
    feat_far,
    masked,
    picked,
):
    rows, feat = feats.shape
    blocks = rows // TILE
    live = count[0]
    me = core[0]
    row_ids = lax.broadcasted_iota(jnp.int32, (rows, feat), 0)
    masked[...] = jnp.where(row_ids < live, feats[...], jnp.zeros_like(feats))
    self_term[...] = mm(masked[...], wself[...])
    slot_on = jnp.broadcast_to(slots[...], (rows, slots.shape[1]))
    cut = cweight[...] * slot_on.astype(BF)
    cut_mask[...] = cut
    deg = jnp.sum(cut.astype(F32), axis=1, keepdims=True)
    deg = deg + jnp.sum(hubw[...].astype(F32), axis=1, keepdims=True)
    lane = lax.broadcasted_iota(jnp.int32, (TILE, TILE), 1)
    for r in range(blocks):
        part = jnp.zeros((TILE, 1), F32)
        at = pl.ds(r * TILE, TILE)
        for t in range(TPR):
            base = cols[r, t] * TILE
            picked[pl.ds(t * TILE, TILE), :] = masked[pl.ds(pl.multiple_of(base, TILE), TILE), :]
            vals = lweight[at, pl.ds(t * TILE, TILE)].astype(F32)
            part = part + jnp.sum(jnp.where(lane + base < live, vals, 0.0), axis=1, keepdims=True)
        local_sum[at, :] = mm(lweight[at, :], picked[...])
        degree[at, :] = part
    degree[...] += deg
    spot = lax.broadcasted_iota(jnp.int32, (slots.shape[1], rows), 0)
    flip = jnp.transpose(cut)
    side = (spot // 4) % 2
    cut_own[...] = jnp.where(side == me, flip, jnp.zeros_like(flip))
    wide = flip.astype(F32)
    count_s = slots.shape[1]
    up = pltpu.roll(wide, count_s - 4, 0)
    down = pltpu.roll(wide, 4, 0)
    moved = jnp.where(me == 0, up, down)
    cut_out[...] = jnp.where(side == me, moved, 0.0).astype(BF)
    half = feat // 2
    feat_own[...] = jnp.transpose(jnp.where(me == 0, feats[:, :half], feats[:, half:]))
    feat_far[...] = jnp.transpose(jnp.where(me == 0, other[:, :half], other[:, half:]))
    step = 128
    hubs = dense.shape[1]

    def build(i, carry):
        base = pl.multiple_of(i * step, step)
        hub = lax.broadcasted_iota(jnp.int32, (step, rows), 0) + base
        acc = jnp.zeros((step, rows), F32)
        for k in range(ids.shape[0]):
            acc = acc + jnp.where(ids[k : k + 1, :] == hub, idw[k : k + 1, :], 0.0)
        flat = acc.astype(BF)
        dense[:, pl.ds(base, step)] = jnp.transpose(flat)

        @pl.when(base < hubs // 2)
        def _():
            flip_own[pl.ds(base, step), :] = flat

        @pl.when(base >= hubs // 2)
        def _():
            flip_out[pl.ds(pl.multiple_of(base - hubs // 2, step), step), :] = flat

        return carry

    lax.fori_loop(0, hubs // step, build, 0)


def mean_near(local_sum, cut_mask, cut_in, dense, table, out):
    hubs = dense.shape[1] // 2
    rows, feat = out.shape
    total = local_sum[...] + mm(cut_mask[...], cut_in[...].reshape(cut_mask.shape[1], feat))
    out[...] = total + mm(dense[:, :hubs], table[...].reshape(hubs, feat))


def mean_far(core, near, dense, table, degree, mean, own, far):
    hubs = dense.shape[1] // 2
    rows, feat = near.shape
    half = feat // 2
    total = near[...] + mm(dense[:, hubs:], table[...].reshape(hubs, feat))
    value = (total / degree[...]).astype(BF)
    mean[...] = value
    me = core[0]
    own[...] = jnp.transpose(jnp.where(me == 0, value[:, :half], value[:, half:]))
    far[...] = jnp.transpose(jnp.where(me == 0, value[:, half:], value[:, :half]))


def gates(count, mean, self_term, wneigh, cot, act, grad):
    rows, feat = mean.shape
    live = lax.broadcasted_iota(jnp.int32, (rows, feat), 0) < count[0]
    pre = self_term[...] + mm(mean[...], wneigh[...])
    sig = jax.nn.sigmoid(pre)
    act[...] = jnp.where(live, pre * sig, 0.0).astype(BF)
    grad[...] = jnp.where(
        live, cot[...].astype(F32) * sig * (1.0 + pre * (1.0 - sig)), 0.0
    ).astype(BF)


def weight_terms(grad, grad_far, feat_own, feat_far, mean_own, mean_pair, out):
    half = feat_own.shape[0]
    peers = out.shape[0]
    first = mm(feat_own[...], grad[...]) + mm(feat_far[...], grad_far[...])
    second = mm(mean_own[...], grad[...]) + mm(mean_pair[...], grad_far[...])
    out[: peers // 2] = first.astype(BF).reshape(peers // 2, *out.shape[1:])
    out[peers // 2 :] = second.astype(BF).reshape(peers // 2, *out.shape[1:])


def back_terms(
    grad, grad_far, wneigh, degree, degree_far, flip_own, flip_far, cut_own, cut_far, gmean, hub_out, cut_out
):
    near = (mm_nt(grad[...], wneigh[...]) / degree[...]).astype(BF)
    far = (mm_nt(grad_far[...], wneigh[...]) / degree_far[...]).astype(BF)
    gmean[...] = near
    hub = mm(flip_own[...], near) + mm(flip_far[...], far)
    hub_out[...] = hub.astype(BF).reshape(hub_out.shape)
    cut = mm(cut_own[...], near) + mm(cut_far[...], far)
    cut_out[...] = cut.astype(BF).reshape(cut_out.shape)


def row_terms(cols, grad, wself, lweight, gmean, out):
    rows, feat = grad.shape
    out[...] = mm_nt(grad[...], wself[...])
    for r in range(rows // TILE):
        at = pl.ds(r * TILE, TILE)
        part = mm_tn(lweight[at, :], gmean[at, :])
        for t in range(TPR):
            base = pl.multiple_of(cols[r, t] * TILE, TILE)
            out[pl.ds(base, TILE), :] += part[t * TILE : (t + 1) * TILE, :]


def finish(count, rows_in, cut_ids, cut_back, hub_ids, hub_back, out):
    rows, feat = rows_in.shape
    slots = cut_ids.shape[1]
    hubs = hub_ids.shape[1]
    top = mm(hot(cut_ids[...], (REACH, slots), 0), cut_back[...].reshape(slots, feat))
    top = top + mm(hot(hub_ids[...], (REACH, hubs), 0), hub_back[...].reshape(hubs, feat))
    live = lax.broadcasted_iota(jnp.int32, (rows, feat), 0) < count[0]
    out[:REACH, :] = jnp.where(live[:REACH], rows_in[:REACH, :] + top, 0.0).astype(BF)
    out[REACH:, :] = jnp.where(live[REACH:], rows_in[REACH:, :], 0.0).astype(BF)


def spread(parts, out):
    total = jnp.sum(parts[...].astype(F32), axis=0)
    out[...] = jnp.broadcast_to(total.astype(BF)[None], out.shape)


def per_device(
    features,
    weight_self,
    weight_neigh,
    local_weight,
    tile_cols,
    cut_weight,
    send_rows,
    send_count,
    hub_rows,
    hub_edges,
    hub_weight,
    row_counts,
    cotangent,
):
    rows, feat = features.shape
    core = lax.axis_index(CORE).astype(jnp.int32)
    chips = lax.axis_size(CHIPS)
    slot_count = send_rows.shape[1]
    hub_dev = hub_rows.shape[0]
    hubs = chips * 2 * hub_dev
    slots = chips * 2 * slot_count
    half = feat // 2
    core_at = core.reshape(1)
    like = lambda shape, kind: jax.ShapeDtypeStruct(shape, kind)
    unit = 2 * 512 * 512 * 512

    (hub_out,) = call(
        hub_send, [like((chips, hub_dev, feat), BF)], [VM, VM], unit // 32, hub_rows.reshape(hub_dev, 1), features
    )
    hub_got = over_chips(hub_out)
    features_far = pair(features)
    routes = send_rows.reshape(chips, 2, slot_count)
    routes_far = pair(send_rows).reshape(chips, 2, slot_count)
    mine = jnp.where(core == 0, routes[:, 0], routes[:, 1])
    theirs = jnp.where(core == 0, routes_far[:, 0], routes_far[:, 1]) + REACH
    sources = jnp.where(
        core == 0, jnp.stack([mine, theirs], axis=1), jnp.stack([theirs, mine], axis=1)
    ).reshape(slots, 1)
    (cut_sent,) = call(
        cut_send, [like((chips, 2 * slot_count, feat), BF)], [VM] * 3, unit, sources, features, features_far
    )
    cut_in = over_chips(cut_sent)

    slot_live = jnp.arange(slot_count, dtype=jnp.int32)[None, :] < send_count
    slot_live = slot_live.astype(F32).reshape(1, slots)
    owner = hub_edges // hub_dev
    place = ((owner % 2) ^ core) * (hubs // 2) + (owner // 2) * hub_dev + hub_edges % hub_dev
    (
        local_sum,
        self_term,
        degree,
        cut_mask,
        dense,
        flip_own,
        flip_out,
        cut_own,
        cut_out,
        feat_own,
        feat_far,
    ) = pl.pallas_call(
        ahead,
        out_shape=(
            like((rows, feat), F32),
            like((rows, feat), F32),
            like((rows, 1), F32),
            like((rows, slots), BF),
            like((rows, hubs), BF),
            like((hubs // 2, rows), BF),
            like((hubs // 2, rows), BF),
            like((slots, rows), BF),
            like((slots, rows), BF),
            like((half, rows), BF),
            like((half, rows), BF),
        ),
        in_specs=[SM, SM, SM] + [VM] * 9,
        out_specs=tuple([VM] * 11),
        scratch_shapes=[pltpu.VMEM((rows, feat), BF), pltpu.VMEM((TPR * TILE, feat), BF)],
        name="ahead",
        cost_estimate=pl.CostEstimate(flops=40 * unit, bytes_accessed=1 << 24, transcendentals=0),
    )(
        tile_cols,
        row_counts,
        core_at,
        features,
        local_weight,
        cut_weight,
        slot_live,
        place.T,
        hub_weight.T.astype(F32),
        hub_weight,
        weight_self,
        features_far,
    )
    degree_far = pair(degree)
    flip_far = pair(flip_out)
    cut_far = pair(cut_out)

    table_far = pair(hub_got)
    (near,) = call(
        mean_near, [like((rows, feat), F32)], [VM] * 5, 3 * unit, local_sum, cut_mask, cut_in, dense, hub_got
    )
    mean, mean_own, mean_out = call(
        mean_far,
        [like((rows, feat), BF), like((half, rows), BF), like((half, rows), BF)],
        [SM] + [VM] * 4,
        2 * unit,
        core_at,
        near,
        dense,
        table_far,
        degree,
    )
    mean_pair = pair(mean_out)
    activated, grad = call(
        gates,
        [like((rows, feat), BF), like((rows, feat), BF)],
        [SM] + [VM] * 4,
        unit,
        row_counts,
        mean,
        self_term,
        weight_neigh,
        cotangent,
    )
    grad_far = pair(grad)

    share = 2 * half // chips
    (weight_out,) = call(
        weight_terms,
        [like((chips, share, feat), BF)],
        [VM] * 6,
        2 * unit,
        grad,
        grad_far,
        feat_own,
        feat_far,
        mean_own,
        mean_pair,
    )
    weight_got = over_chips(weight_out)

    gmean, hub_back, cut_back = call(
        back_terms,
        [like((rows, feat), BF), like((chips, hub_dev, feat), BF), like((chips, 2 * slot_count, feat), BF)],
        [VM] * 9,
        8 * unit,
        grad,
        grad_far,
        weight_neigh,
        degree,
        degree_far,
        flip_own,
        flip_far,
        cut_own,
        cut_far,
    )
    hub_home = over_chips(hub_back)
    cut_home = over_chips(cut_back)
    (weight_sum,) = call(spread, [like((chips, share, feat), BF)], [VM], 1 << 20, weight_got)
    weight_all = over_chips(weight_sum).reshape(2, half, feat)
    weight_pair = pair(weight_all)
    (row_sum,) = call(
        row_terms, [like((rows, feat), F32)], [SM] + [VM] * 4, 3 * unit, tile_cols, grad, weight_self, local_weight, gmean
    )
    hub_spots = jnp.broadcast_to(hub_rows[None, :], (chips, hub_dev)).reshape(1, chips * hub_dev)
    (feature_grad,) = call(
        finish,
        [like((rows, feat), BF)],
        [SM] + [VM] * 5,
        2 * unit,
        row_counts,
        row_sum,
        send_rows.reshape(1, slots),
        cut_home,
        hub_spots,
        hub_home,
    )
    low = jnp.where(core == 0, weight_all, weight_pair).astype(F32)
    high = jnp.where(core == 0, weight_pair, weight_all).astype(F32)
    both = jnp.concatenate([low, high], axis=1)
    return activated, feature_grad, both[0], both[1]


def solution(mesh):
    finer = Mesh(mesh.devices.reshape(4, 4, 4, 2), DOM)
    in_specs = (
        P(DOM, None),
        P(),
        P(),
        P(DOM, None),
        P(DOM, None),
        P(DOM, None),
        P(DOM, None),
        P(None, DOM),
        P(DOM),
        P(DOM, None),
        P(DOM, None),
        P(DOM),
        P(DOM, None),
    )
    out_specs = (P(DOM, None), P(DOM, None), P(), P())
    return jax.shard_map(
        per_device, mesh=finer, in_specs=in_specs, out_specs=out_specs, check_vma=False
    )
```

```python
import jax
import jax.numpy as jnp
from jax import lax
from jax.experimental import pallas as pl
from jax.experimental.pallas import tpu as pltpu
from jax.sharding import Mesh
from jax.sharding import PartitionSpec as P


TILE = 128
TPR = 4
DOM = ("dom_0", "dom_1", "dom_2", "dom_3")
CHIPS = DOM[:3]
CORE = "dom_3"
BF = jnp.bfloat16
F32 = jnp.float32
REACH = 256


VM = pl.BlockSpec(memory_space=pltpu.VMEM)
SM = pl.BlockSpec(memory_space=pltpu.SMEM)
LIMIT = 8 << 20


def call(body, outs, specs, flops, *args, scratch=()):
    size = sum(a.size * a.dtype.itemsize for a in args)
    size += sum(o.size * o.dtype.itemsize for o in outs)
    return pl.pallas_call(
        body,
        out_shape=tuple(outs),
        in_specs=list(specs),
        out_specs=tuple([VM] * len(outs)),
        scratch_shapes=list(scratch),
        compiler_params=pltpu.CompilerParams(vmem_limit_bytes=LIMIT),
        cost_estimate=pl.CostEstimate(flops=flops, bytes_accessed=size, transcendentals=0),
    )(*args)


def mm(a, b):
    return jnp.dot(a, b, preferred_element_type=F32)


def mm_nt(a, b):
    return lax.dot_general(a, b, (((1,), (1,)), ((), ())), preferred_element_type=F32)


def mm_tn(a, b):
    return lax.dot_general(a, b, (((0,), (0,)), ((), ())), preferred_element_type=F32)


def pair(x):
    return lax.ppermute(x, CORE, [(0, 1), (1, 0)])


def over_chips(x):
    return lax.all_to_all(x, CHIPS, 0, 0, tiled=True)


def iota(shape, dim):
    return lax.broadcasted_iota(jnp.int32, shape, dim)


def ones_where(cond):
    return jnp.where(cond, 1.0, 0.0).astype(BF)


def small(ids):
    return ids.astype(F32).astype(BF)


def across(table, width):
    deep, peers = table.shape
    fan = ones_where(iota((peers, width), 0) == iota((peers, width), 1) // deep)
    wide = mm(small(table), fan)
    keep = iota((deep, width), 0) == iota((deep, width), 1) % deep
    return jnp.sum(jnp.where(keep, wide, 0.0), axis=0, keepdims=True)


def send(routes, hub_ids, feats, out):
    feat = feats.shape[1]
    deep, peers = routes.shape
    slots = deep * peers
    width = hub_ids.shape[1]
    same = iota((width, width), 0) == iota((width, width), 1)
    hub = jnp.sum(jnp.where(same, hub_ids[...].astype(F32), 0.0), axis=1, keepdims=True)
    slab = mm(ones_where(hub.astype(jnp.int32) == iota((width, REACH), 1)), feats[:REACH, :])
    out[:, :width, :] = jnp.broadcast_to(slab.astype(BF)[None], (out.shape[0], width, feat))
    fan = ones_where(iota((slots, peers), 1) == iota((slots, peers), 0) // deep)
    wide = mm_nt(fan, small(routes[...]))
    keep = iota((slots, deep), 1) == iota((slots, deep), 0) % deep
    row = jnp.sum(jnp.where(keep, wide, 0.0), axis=1, keepdims=True).astype(jnp.int32)
    rows = mm(ones_where(row == iota((slots, REACH), 1)), feats[:REACH, :])
    out[:, width:, :] = rows.astype(BF).reshape(out.shape[0], slots // out.shape[0], feat)


def ahead(
    cols,
    count,
    core,
    feats,
    lweight,
    cweight,
    counts,
    edges,
    hubw,
    wself,
    local_sum,
    self_term,
    degree,
    dense,
    flip_own,
    cut_own,
    wide_own,
    wide_far,
    feat_own,
    ship,
    masked,
    picked,
):
    rows, feat = feats.shape
    slots = cweight.shape[1]
    hubs = dense.shape[1]
    blocks = rows // TILE
    live = count[0]
    me = core[0]
    masked[...] = jnp.where(iota((rows, feat), 0) < live, feats[...], jnp.zeros_like(feats))
    self_term[...] = mm(masked[...], wself[...])
    deep = slots // counts.shape[1]
    fan = ones_where(iota((counts.shape[1], slots), 0) == iota((counts.shape[1], slots), 1) // deep)
    used = mm(small(counts[...]), fan)
    on = (iota((1, slots), 1) % deep).astype(F32) < used
    cut = cweight[...] * jnp.broadcast_to(ones_where(on), (rows, slots))
    edge_w = hubw[...]
    hub_deg = mm_tn(edge_w, jnp.ones((edge_w.shape[0], TILE), BF))[:, :1]
    degree[...] = hub_deg + jnp.sum(cut.astype(F32), axis=1, keepdims=True)
    lane = iota((TILE, TILE), 1)
    for r in range(blocks):
        part = jnp.zeros((TILE, 1), F32)
        at = pl.ds(r * TILE, TILE)
        for t in range(TPR):
            base = cols[r, t] * TILE
            picked[pl.ds(t * TILE, TILE), :] = masked[pl.ds(pl.multiple_of(base, TILE), TILE), :]
            vals = lweight[at, pl.ds(t * TILE, TILE)].astype(F32)
            part = part + jnp.sum(jnp.where(lane + base < live, vals, 0.0), axis=1, keepdims=True)
        local_sum[at, :] = mm(lweight[at, :], picked[...])
        degree[at, :] += part
    flip = jnp.transpose(cut)
    side = (iota((slots, rows), 0) // deep) % 2
    kept = jnp.where(side == me, flip, jnp.zeros_like(flip))
    tall = flip.astype(F32)
    up = pltpu.roll(tall, slots - deep, 0)
    down = pltpu.roll(tall, deep, 0)
    moved = jnp.where(side == me, jnp.where(me == 0, up, down), 0.0).astype(BF)
    cut_own[...] = kept
    wide_own[...] = jnp.transpose(kept)
    wide_far[...] = jnp.transpose(moved)
    half = feat // 2
    ship[hubs // 2 : hubs // 2 + slots, :] = moved
    feat_own[...] = jnp.transpose(jnp.where(me == 0, feats[:, :half], feats[:, half:]))
    ship[hubs // 2 + slots :, :] = jnp.transpose(
        jnp.where(me == 0, feats[:, half:], feats[:, :half])
    )
    width = hubs // (2 * (slots // (2 * deep)))
    owner = edges[...] // width
    place = ((owner % 2) ^ me) * (hubs // 2) + (owner // 2) * width + edges[...] % width
    weight = edge_w.astype(F32)
    step = 128

    def build(i, carry):
        base = pl.multiple_of(i * step, step)
        hub = iota((step, rows), 0) + base
        acc = jnp.zeros((step, rows), F32)
        for k in range(edges.shape[0]):
            acc = acc + jnp.where(place[k : k + 1, :] == hub, weight[k : k + 1, :], 0.0)
        flat = acc.astype(BF)
        dense[:, pl.ds(base, step)] = jnp.transpose(flat)

        @pl.when(base < hubs // 2)
        def _():
            flip_own[pl.ds(base, step), :] = flat

        @pl.when(base >= hubs // 2)
        def _():
            ship[pl.ds(pl.multiple_of(base - hubs // 2, step), step), :] = flat

        return carry

    lax.fori_loop(0, hubs // step, build, 0)


def sides(bundle, width, feat):
    peers, deep, _ = bundle.shape
    table = bundle[:, :width, :].reshape(peers * width, feat)
    return table, bundle[:, width:, :].reshape(peers * (deep - width), feat)


def near_sum(local_sum, wide_own, dense, bundle, out):
    _, feat = out.shape
    hubs = dense.shape[1] // 2
    table, cut = sides(bundle, hubs // bundle.shape[0], feat)
    out[...] = local_sum[...] + mm(wide_own[...], cut) + mm(dense[:, :hubs], table)


def forward(core, count, near, wide_far, dense, bundle, degree, self_term, wneigh, cot, act, mean_own, pack):
    rows, feat = near.shape
    hubs = dense.shape[1] // 2
    half = feat // 2
    me = core[0]
    table, cut = sides(bundle, hubs // bundle.shape[0], feat)
    total = near[...] + mm(wide_far[...], cut) + mm(dense[:, hubs:], table)
    mean = (total / degree[...]).astype(BF)
    mean_own[...] = jnp.transpose(jnp.where(me == 0, mean[:, :half], mean[:, half:]))
    pack[:half, :] = jnp.transpose(jnp.where(me == 0, mean[:, half:], mean[:, :half]))
    live = iota((rows, feat), 0) < count[0]
    pre = self_term[...] + mm(mean, wneigh[...])
    sig = jax.nn.sigmoid(pre)
    act[...] = jnp.where(live, pre * sig, 0.0).astype(BF)
    grad = cot[...].astype(F32) * sig * (1.0 + pre * (1.0 - sig))
    pack[half:, :] = jnp.where(live, grad, 0.0).astype(BF)


def back_near(pack, mean_own, feat_own, wneigh, degree, flip_own, cut_own, gmean, hub, cut, weight):
    half = feat_own.shape[0]
    grad = pack[half:, :]
    near = (mm_nt(grad, wneigh[...]) / degree[...]).astype(BF)
    gmean[...] = near
    hub[...] = mm(flip_own[...], near)
    cut[...] = mm(cut_own[...], near)
    weight[:half, :] = mm(feat_own[...], grad)
    weight[half:, :] = mm(mean_own[...], grad)


def back_far(pack, wneigh, degree, ship, hub, cut, weight, out):
    feat = wneigh.shape[0]
    half = feat // 2
    grad = pack[half:, :]
    hubs, slots = hub.shape[0], cut.shape[0]
    peers = out.shape[0]
    a, b = hubs // peers, (hubs + slots) // peers
    far = (mm_nt(grad, wneigh[...]) / degree[...]).astype(BF)
    first = hub[...] + mm(ship[:hubs, :], far)
    out[:, :a, :] = first.astype(BF).reshape(peers, a, feat)
    second = cut[...] + mm(ship[hubs : hubs + slots, :], far)
    out[:, a:b, :] = second.astype(BF).reshape(peers, b - a, feat)
    share = feat // peers
    low = weight[:half, :] + mm(ship[hubs + slots :, :], grad)
    high = weight[half:, :] + mm(pack[:half, :], grad)
    out[: peers // 2, b:, :] = low.astype(BF).reshape(peers // 2, share, feat)
    out[peers // 2 :, b:, :] = high.astype(BF).reshape(peers // 2, share, feat)


def row_terms(cols, pack, wself, lweight, gmean, out):
    rows, feat = out.shape
    out[...] = mm_nt(pack[feat // 2 :, :], wself[...])
    for r in range(rows // TILE):
        at = pl.ds(r * TILE, TILE)
        part = mm_tn(lweight[at, :], gmean[at, :])
        for t in range(TPR):
            base = pl.multiple_of(cols[r, t] * TILE, TILE)
            out[pl.ds(base, TILE), :] += part[t * TILE : (t + 1) * TILE, :]


def spread(bundle, out):
    share = out.shape[1]
    first = bundle.shape[1] - share
    total = jnp.sum(bundle[:, first:, :].astype(F32), axis=0)
    out[...] = jnp.broadcast_to(total.astype(BF)[None], out.shape)


def finish(count, rows_in, routes, hub_ids, bundle, out):
    rows, feat = rows_in.shape
    deep, peers = routes.shape
    slots = deep * peers
    chips = bundle.shape[0]
    width = hub_ids.shape[1]
    hubs = chips * width
    ids = across(routes[...], slots).astype(jnp.int32)
    cut = bundle[:, width : width + slots // chips, :].reshape(slots, feat)
    top = mm(ones_where(ids == iota((REACH, slots), 0)), cut)
    fan = ones_where(iota((width, hubs), 0) == iota((width, hubs), 1) % width)
    spots = mm(small(hub_ids[...]), fan).astype(jnp.int32)
    table = bundle[:, :width, :].reshape(hubs, feat)
    top = top + mm(ones_where(spots == iota((REACH, hubs), 0)), table)
    live = iota((rows, feat), 0) < count[0]
    out[:REACH, :] = jnp.where(live[:REACH], rows_in[:REACH, :] + top, 0.0).astype(BF)
    out[REACH:, :] = jnp.where(live[REACH:], rows_in[REACH:, :], 0.0).astype(BF)


def assemble(core, mine, other, first, second):
    peers, share, feat = mine.shape
    half = peers * share // 2
    me = core[0]
    for source, turn in ((mine, me), (other, 1 - me)):
        whole = source[...].reshape(peers * share, feat).astype(F32)
        at = pl.ds(pl.multiple_of(turn * half, half), half)
        first[at, :] = whole[:half, :]
        second[at, :] = whole[half:, :]


def per_device(
    features,
    weight_self,
    weight_neigh,
    local_weight,
    tile_cols,
    cut_weight,
    send_rows,
    send_count,
    hub_rows,
    hub_edges,
    hub_weight,
    row_counts,
    cotangent,
):
    rows, feat = features.shape
    core = lax.axis_index(CORE).astype(jnp.int32).reshape(1)
    chips = lax.axis_size(CHIPS)
    deep = send_rows.shape[1]
    width = hub_rows.shape[0]
    hubs = chips * 2 * width
    slots = chips * 2 * deep
    half = feat // 2
    share = feat // chips
    unit = 2 * 512 * 512 * 512

    def like(shape, kind=BF):
        return jax.ShapeDtypeStruct(shape, kind)

    routes = send_rows.T
    hub_ids = hub_rows.reshape(1, width)
    (bundle,) = call(
        send, [like((chips, width + 2 * deep, feat))], [VM] * 3, unit, routes, hub_ids, features
    )
    bundle = over_chips(bundle)
    (
        local_sum,
        self_term,
        degree,
        dense,
        flip_own,
        cut_own,
        wide_own,
        wide_far,
        feat_own,
        ship,
    ) = call(
        ahead,
        [
            like((rows, feat), F32),
            like((rows, feat), F32),
            like((rows, 1), F32),
            like((rows, hubs)),
            like((hubs // 2, rows)),
            like((slots, rows)),
            like((rows, slots)),
            like((rows, slots)),
            like((half, rows)),
            like((hubs // 2 + slots + half, rows)),
        ],
        [SM, SM, SM] + [VM] * 7,
        40 * unit,
        tile_cols,
        row_counts,
        core,
        features,
        local_weight,
        cut_weight,
        send_count.T,
        hub_edges.T,
        hub_weight.T,
        weight_self,
        scratch=[pltpu.VMEM((rows, feat), BF), pltpu.VMEM((TPR * TILE, feat), BF)],
    )
    degree_far = pair(degree)
    ship_far = pair(ship)

    bundle_far = pair(bundle)
    (near,) = call(near_sum, [like((rows, feat), F32)], [VM] * 4, 3 * unit, local_sum, wide_own, dense, bundle)
    activated, mean_own, pack = call(
        forward,
        [like((rows, feat)), like((half, rows)), like((half + rows, feat))],
        [SM, SM] + [VM] * 8,
        4 * unit,
        core,
        row_counts,
        near,
        wide_far,
        dense,
        bundle_far,
        degree,
        self_term,
        weight_neigh,
        cotangent,
    )
    pack_far = pair(pack)
    gmean, hub_part, cut_part, weight_part = call(
        back_near,
        [like((rows, feat)), like((hubs // 2, feat), F32), like((slots, feat), F32), like((feat, feat), F32)],
        [VM] * 7,
        5 * unit,
        pack,
        mean_own,
        feat_own,
        weight_neigh,
        degree,
        flip_own,
        cut_own,
    )
    (back,) = call(
        back_far,
        [like((chips, width + 2 * deep + share, feat))],
        [VM] * 7,
        5 * unit,
        pack_far,
        weight_neigh,
        degree_far,
        ship_far,
        hub_part,
        cut_part,
        weight_part,
    )
    back = over_chips(back)
    (row_sum,) = call(
        row_terms, [like((rows, feat), F32)], [SM] + [VM] * 4, 3 * unit, tile_cols, pack, weight_self, local_weight, gmean
    )
    (weight_sum,) = call(spread, [like((chips, share, feat))], [VM], 1 << 20, back)
    weight_all = over_chips(weight_sum)
    weight_pair = pair(weight_all)
    (feature_grad,) = call(
        finish,
        [like((rows, feat))],
        [SM] + [VM] * 4,
        2 * unit,
        row_counts,
        row_sum,
        routes,
        hub_ids,
        back,
    )
    grad_self, grad_neigh = call(
        assemble, [like((feat, feat), F32)] * 2, [SM, VM, VM], 1 << 20, core, weight_all, weight_pair
    )
    return activated, feature_grad, grad_self, grad_neigh


def solution(mesh):
    finer = Mesh(mesh.devices.reshape(4, 4, 4, 2), DOM)
    in_specs = (
        P(DOM, None),
        P(),
        P(),
        P(DOM, None),
        P(DOM, None),
        P(DOM, None),
        P(DOM, None),
        P(None, DOM),
        P(DOM),
        P(DOM, None),
        P(DOM, None),
        P(DOM),
        P(DOM, None),
    )
    out_specs = (P(DOM, None), P(DOM, None), P(), P())

    return jax.shard_map(
        per_device, mesh=finer, in_specs=in_specs, out_specs=out_specs, check_vma=False
    )
```

```python
import jax
import jax.numpy as jnp
from jax import lax
from jax.experimental import pallas as pl
from jax.experimental.pallas import tpu as pltpu
from jax.sharding import Mesh
from jax.sharding import PartitionSpec as P


TILE = 128
TPR = 4
DOM = ("dom_0", "dom_1", "dom_2", "dom_3")
CHIPS = DOM[:3]
CORE = "dom_3"
BF = jnp.bfloat16
F32 = jnp.float32
REACH = 256


VM = pl.BlockSpec(memory_space=pltpu.VMEM)
SM = pl.BlockSpec(memory_space=pltpu.SMEM)
HB = pl.BlockSpec(memory_space=pltpu.MemorySpace.HBM)
DMA = pltpu.SemaphoreType.DMA
LIMIT = 8 << 20


def call(body, outs, specs, flops, *args, scratch=(), to=None, alias=None):
    size = sum(a.size * a.dtype.itemsize for a in args)
    size += sum(o.size * o.dtype.itemsize for o in outs)
    spaces = to or [VM] * len(outs)
    return pl.pallas_call(
        body,
        out_shape=tuple(
            pltpu.MemorySpace.HBM(o.shape, o.dtype) if p is HB else o for o, p in zip(outs, spaces)
        ),
        in_specs=list(specs),
        out_specs=tuple(spaces),
        scratch_shapes=list(scratch),
        input_output_aliases=alias or {},
        compiler_params=pltpu.CompilerParams(vmem_limit_bytes=LIMIT),
        cost_estimate=pl.CostEstimate(flops=flops, bytes_accessed=size, transcendentals=0),
    )(*args)


def mm(a, b):
    return jnp.dot(a, b, preferred_element_type=F32)


def mm_nt(a, b):
    return lax.dot_general(a, b, (((1,), (1,)), ((), ())), preferred_element_type=F32)


def mm_tn(a, b):
    return lax.dot_general(a, b, (((0,), (0,)), ((), ())), preferred_element_type=F32)


def pair(x):
    return lax.ppermute(x, CORE, [(0, 1), (1, 0)])


def over_chips(x):
    return lax.all_to_all(x, CHIPS, 0, 0, tiled=True)


def iota(shape, dim):
    return lax.broadcasted_iota(jnp.int32, shape, dim)


def ones_where(cond):
    return jnp.where(cond, 1.0, 0.0).astype(BF)


def small(ids):
    return ids.astype(F32).astype(BF)


def across(table, width):
    deep, peers = table.shape
    fan = ones_where(iota((peers, width), 0) == iota((peers, width), 1) // deep)
    wide = mm(small(table), fan)
    keep = iota((deep, width), 0) == iota((deep, width), 1) % deep
    return jnp.sum(jnp.where(keep, wide, 0.0), axis=0, keepdims=True)


def send(routes_at, hub_ids_at, feats_at, out, routes, hub_ids, feats, hubs_out, cuts_out, sem):
    reads = [
        pltpu.make_async_copy(routes_at, routes, sem.at[0]),
        pltpu.make_async_copy(hub_ids_at, hub_ids, sem.at[1]),
        pltpu.make_async_copy(feats_at.at[pl.ds(0, REACH)], feats, sem.at[2]),
    ]
    for read in reads:
        read.start()
    for read in reads:
        read.wait()
    deep, peers = routes.shape
    slots = deep * peers
    width = hub_ids.shape[1]
    same = iota((width, width), 0) == iota((width, width), 1)
    hub = jnp.sum(jnp.where(same, hub_ids[...].astype(F32), 0.0), axis=1, keepdims=True)
    slab = mm(ones_where(hub.astype(jnp.int32) == iota((width, REACH), 1)), feats[...])
    hubs_out[...] = jnp.broadcast_to(slab.astype(BF)[None], hubs_out.shape)
    first = pltpu.make_async_copy(hubs_out, out.at[:, pl.ds(0, width), :], sem.at[3])
    first.start()
    fan = ones_where(iota((slots, peers), 1) == iota((slots, peers), 0) // deep)
    wide = mm_nt(fan, small(routes[...]))
    keep = iota((slots, deep), 1) == iota((slots, deep), 0) % deep
    row = jnp.sum(jnp.where(keep, wide, 0.0), axis=1, keepdims=True).astype(jnp.int32)
    rows = mm(ones_where(row == iota((slots, REACH), 1)), feats[...])
    cuts_out[...] = rows.astype(BF).reshape(cuts_out.shape)
    second = pltpu.make_async_copy(
        cuts_out, out.at[:, pl.ds(width, cuts_out.shape[1]), :], sem.at[4]
    )
    second.start()
    first.wait()
    second.wait()


def ahead(
    cols,
    count,
    core,
    feats,
    lweight,
    cweight,
    counts,
    edges,
    hubw,
    wself,
    local_sum,
    self_term,
    degree,
    dense,
    dense_far,
    flip_own,
    cut_own,
    wide_own,
    wide_far,
    feat_own,
    ship,
    masked,
    picked,
):
    rows, feat = feats.shape
    slots = cweight.shape[1]
    hubs = 2 * dense.shape[1]
    blocks = rows // TILE
    live = count[0]
    me = core[0]
    masked[...] = jnp.where(iota((rows, feat), 0) < live, feats[...], jnp.zeros_like(feats))
    self_term[...] = mm(masked[...], wself[...])
    deep = slots // counts.shape[1]
    fan = ones_where(iota((counts.shape[1], slots), 0) == iota((counts.shape[1], slots), 1) // deep)
    used = mm(small(counts[...]), fan)
    on = (iota((1, slots), 1) % deep).astype(F32) < used
    cut = cweight[...] * jnp.broadcast_to(ones_where(on), (rows, slots))
    edge_w = hubw[...]
    hub_deg = mm_tn(edge_w, jnp.ones((edge_w.shape[0], TILE), BF))[:, :1]
    degree[...] = hub_deg + jnp.sum(cut.astype(F32), axis=1, keepdims=True)
    lane = iota((TILE, TILE), 1)
    for r in range(blocks):
        part = jnp.zeros((TILE, 1), F32)
        at = pl.ds(r * TILE, TILE)
        for t in range(TPR):
            base = cols[r, t] * TILE
            picked[pl.ds(t * TILE, TILE), :] = masked[pl.ds(pl.multiple_of(base, TILE), TILE), :]
            vals = lweight[at, pl.ds(t * TILE, TILE)].astype(F32)
            part = part + jnp.sum(jnp.where(lane + base < live, vals, 0.0), axis=1, keepdims=True)
        local_sum[at, :] = mm(lweight[at, :], picked[...])
        degree[at, :] += part
    flip = jnp.transpose(cut)
    side = (iota((slots, rows), 0) // deep) % 2
    kept = jnp.where(side == me, flip, jnp.zeros_like(flip))
    tall = flip.astype(F32)
    up = pltpu.roll(tall, slots - deep, 0)
    down = pltpu.roll(tall, deep, 0)
    moved = jnp.where(side == me, jnp.where(me == 0, up, down), 0.0).astype(BF)
    cut_own[...] = kept
    wide_own[...] = jnp.transpose(kept)
    wide_far[...] = jnp.transpose(moved)
    half = feat // 2
    ship[hubs // 2 : hubs // 2 + slots, :] = moved
    feat_own[...] = jnp.transpose(jnp.where(me == 0, feats[:, :half], feats[:, half:]))
    ship[hubs // 2 + slots :, :] = jnp.transpose(
        jnp.where(me == 0, feats[:, half:], feats[:, :half])
    )
    width = hubs // (2 * (slots // (2 * deep)))
    owner = edges[...] // width
    place = ((owner % 2) ^ me) * (hubs // 2) + (owner // 2) * width + edges[...] % width
    weight = edge_w.astype(F32)
    step = 128

    def build(i, carry):
        base = pl.multiple_of(i * step, step)
        hub = iota((step, rows), 0) + base
        acc = jnp.zeros((step, rows), F32)
        for k in range(edges.shape[0]):
            acc = acc + jnp.where(place[k : k + 1, :] == hub, weight[k : k + 1, :], 0.0)
        flat = acc.astype(BF)

        @pl.when(base < hubs // 2)
        def _():
            flip_own[pl.ds(base, step), :] = flat
            dense[:, pl.ds(base, step)] = jnp.transpose(flat)

        @pl.when(base >= hubs // 2)
        def _():
            spot = pl.multiple_of(base - hubs // 2, step)
            ship[pl.ds(spot, step), :] = flat
            dense_far[:, pl.ds(spot, step)] = jnp.transpose(flat)

        return carry

    lax.fori_loop(0, hubs // step, build, 0)


def sides(bundle, width, feat):
    peers, deep, _ = bundle.shape
    table = bundle[:, :width, :].reshape(peers * width, feat)
    return table, bundle[:, width:, :].reshape(peers * (deep - width), feat)


def near_sum(wide_own, dense, bundle, out):
    _, feat = out.shape
    table, cut = sides(bundle, dense.shape[1] // bundle.shape[0], feat)
    out[...] = mm(wide_own[...], cut) + mm(dense[...], table)


def forward(
    core, count, near, local_sum, wide_far, dense, bundle, degree, self_term, wneigh, cot, act, mean_own, pack
):
    rows, feat = near.shape
    half = feat // 2
    me = core[0]
    table, cut = sides(bundle, dense.shape[1] // bundle.shape[0], feat)
    total = local_sum[...] + near[...] + mm(wide_far[...], cut) + mm(dense[...], table)
    mean = (total / degree[...]).astype(BF)
    mean_own[...] = jnp.transpose(jnp.where(me == 0, mean[:, :half], mean[:, half:]))
    pack[:half, :] = jnp.transpose(jnp.where(me == 0, mean[:, half:], mean[:, :half]))
    live = iota((rows, feat), 0) < count[0]
    pre = self_term[...] + mm(mean, wneigh[...])
    sig = jax.nn.sigmoid(pre)
    act[...] = jnp.where(live, pre * sig, 0.0).astype(BF)
    grad = cot[...].astype(F32) * sig * (1.0 + pre * (1.0 - sig))
    pack[half:, :] = jnp.where(live, grad, 0.0).astype(BF)


def back_near(pack, wneigh, degree, flip_own, cut_own, gmean, hub, cut, near, sem):
    half = wneigh.shape[0] // 2
    near[...] = (mm_nt(pack[half:, :], wneigh[...]) / degree[...]).astype(BF)
    away = pltpu.make_async_copy(near, gmean, sem)
    away.start()
    hub[...] = mm(flip_own[...], near[...])
    cut[...] = mm(cut_own[...], near[...])
    away.wait()


def weight_near(pack, mean_own, feat_own, out):
    half = feat_own.shape[0]
    grad = pack[half:, :]
    out[:half, :] = mm(feat_own[...], grad)
    out[half:, :] = mm(mean_own[...], grad)


def back_far(pack, wneigh, degree, ship, hub, cut, weight, out, hubs_out, cuts_out, weights_out, sem):
    feat = wneigh.shape[0]
    half = feat // 2
    hubs, slots = hub.shape[0], cut.shape[0]
    width, deep, share = hubs_out.shape[1], cuts_out.shape[1], weights_out.shape[1]
    peers = out.shape[0]
    grad = pack[half:, :]
    far = (mm_nt(grad, wneigh[...]) / degree[...]).astype(BF)
    first = hub[...] + mm(ship[:hubs, :], far)
    hubs_out[...] = first.astype(BF).reshape(hubs_out.shape)
    one = pltpu.make_async_copy(hubs_out, out.at[:, pl.ds(0, width), :], sem.at[0])
    one.start()
    second = cut[...] + mm(ship[hubs : hubs + slots, :], far)
    cuts_out[...] = second.astype(BF).reshape(cuts_out.shape)
    two = pltpu.make_async_copy(cuts_out, out.at[:, pl.ds(width, deep), :], sem.at[1])
    two.start()
    low = weight[:half, :] + mm(ship[hubs + slots :, :], grad)
    weights_out[: peers // 2] = low.astype(BF).reshape(peers // 2, share, feat)
    high = weight[half:, :] + mm(pack[:half, :], grad)
    weights_out[peers // 2 :] = high.astype(BF).reshape(peers // 2, share, feat)
    three = pltpu.make_async_copy(weights_out, out.at[:, pl.ds(width + deep, share), :], sem.at[2])
    three.start()
    one.wait()
    two.wait()
    three.wait()


def row_terms(cols, pack, wself, lweight, gmean, out):
    rows, feat = out.shape
    out[...] = mm_nt(pack[feat // 2 :, :], wself[...])
    for r in range(rows // TILE):
        at = pl.ds(r * TILE, TILE)
        part = mm_tn(lweight[at, :], gmean[at, :])
        for t in range(TPR):
            base = pl.multiple_of(cols[r, t] * TILE, TILE)
            out[pl.ds(base, TILE), :] += part[t * TILE : (t + 1) * TILE, :]


def spread(parts, out, held, sem):
    share = held.shape[1]
    first = parts.shape[1] - share
    total = jnp.sum(parts[:, first:, :].astype(F32), axis=0)
    held[...] = jnp.broadcast_to(total.astype(BF)[None], held.shape)
    away = pltpu.make_async_copy(held, out, sem)
    away.start()
    away.wait()


def finish(count, rows_in, routes, hub_ids, bundle, out):
    rows, feat = rows_in.shape
    deep, peers = routes.shape
    slots = deep * peers
    chips = bundle.shape[0]
    width = hub_ids.shape[1]
    hubs = chips * width
    ids = across(routes[...], slots).astype(jnp.int32)
    cut = bundle[:, width : width + slots // chips, :].reshape(slots, feat)
    top = mm(ones_where(ids == iota((REACH, slots), 0)), cut)
    fan = ones_where(iota((width, hubs), 0) == iota((width, hubs), 1) % width)
    spots = mm(small(hub_ids[...]), fan).astype(jnp.int32)
    table = bundle[:, :width, :].reshape(hubs, feat)
    top = top + mm(ones_where(spots == iota((REACH, hubs), 0)), table)
    live = iota((rows, feat), 0) < count[0]
    out[:REACH, :] = jnp.where(live[:REACH], rows_in[:REACH, :] + top, 0.0).astype(BF)
    out[REACH:, :] = jnp.where(live[REACH:], rows_in[REACH:, :], 0.0).astype(BF)


def place_rows(turn, source, first, second, held, sem):
    half, feat = held.shape[1:]
    whole = source[...].reshape(2 * half, feat).astype(F32)
    at = pl.ds(pl.multiple_of(turn * half, half), half)
    held[0] = whole[:half, :]
    one = pltpu.make_async_copy(held.at[0], first.at[at], sem.at[0])
    one.start()
    held[1] = whole[half:, :]
    two = pltpu.make_async_copy(held.at[1], second.at[at], sem.at[1])
    two.start()
    one.wait()
    two.wait()


def place_own(core, source, first, second, held, sem):
    place_rows(core[0], source, first, second, held, sem)


def place_far(core, source, first_in, second_in, first, second, held, sem):
    place_rows(1 - core[0], source, first, second, held, sem)


def per_device(
    features,
    weight_self,
    weight_neigh,
    local_weight,
    tile_cols,
    cut_weight,
    send_rows,
    send_count,
    hub_rows,
    hub_edges,
    hub_weight,
    row_counts,
    cotangent,
):
    rows, feat = features.shape
    core = lax.axis_index(CORE).astype(jnp.int32).reshape(1)
    chips = lax.axis_size(CHIPS)
    deep = send_rows.shape[1]
    width = hub_rows.shape[0]
    hubs = chips * 2 * width
    slots = chips * 2 * deep
    half = feat // 2
    share = feat // chips
    unit = 2 * 512 * 512 * 512

    def like(shape, kind=BF):
        return jax.ShapeDtypeStruct(shape, kind)

    routes = send_rows.T
    hub_ids = hub_rows.reshape(1, width)
    (bundle,) = call(
        send,
        [like((chips, width + 2 * deep, feat))],
        [HB] * 3,
        unit,
        *[pltpu.with_memory_space_constraint(x, pltpu.MemorySpace.HBM) for x in (routes, hub_ids, features)],
        to=[HB],
        scratch=[
            pltpu.VMEM(routes.shape, routes.dtype),
            pltpu.VMEM(hub_ids.shape, hub_ids.dtype),
            pltpu.VMEM((REACH, feat), BF),
            pltpu.VMEM((chips, width, feat), BF),
            pltpu.VMEM((chips, 2 * deep, feat), BF),
            DMA((5,)),
        ],
    )
    bundle = over_chips(bundle)
    (
        local_sum,
        self_term,
        degree,
        dense,
        dense_far,
        flip_own,
        cut_own,
        wide_own,
        wide_far,
        feat_own,
        ship,
    ) = call(
        ahead,
        [
            like((rows, feat), F32),
            like((rows, feat), F32),
            like((rows, 1), F32),
            like((rows, hubs // 2)),
            like((rows, hubs // 2)),
            like((hubs // 2, rows)),
            like((slots, rows)),
            like((rows, slots)),
            like((rows, slots)),
            like((half, rows)),
            like((hubs // 2 + slots + half, rows)),
        ],
        [SM, SM, SM] + [VM] * 7,
        40 * unit,
        tile_cols,
        row_counts,
        core,
        features,
        local_weight,
        cut_weight,
        send_count.T,
        hub_edges.T,
        hub_weight.T,
        weight_self,
        scratch=[pltpu.VMEM((rows, feat), BF), pltpu.VMEM((TPR * TILE, feat), BF)],
    )
    degree_far = pair(degree)
    ship_far = pair(ship)

    bundle_far = pair(bundle)
    (near,) = call(near_sum, [like((rows, feat), F32)], [VM] * 3, 3 * unit, wide_own, dense, bundle)
    activated, mean_own, pack = call(
        forward,
        [like((rows, feat)), like((half, rows)), like((half + rows, feat))],
        [SM, SM] + [VM] * 9,
        4 * unit,
        core,
        row_counts,
        near,
        local_sum,
        wide_far,
        dense_far,
        bundle_far,
        degree,
        self_term,
        weight_neigh,
        cotangent,
    )
    pack_far = pair(pack)
    gmean, hub_part, cut_part = call(
        back_near,
        [like((rows, feat)), like((hubs // 2, feat), F32), like((slots, feat), F32)],
        [VM] * 5,
        4 * unit,
        pack,
        weight_neigh,
        degree,
        flip_own,
        cut_own,
        to=[HB, VM, VM],
        scratch=[pltpu.VMEM((rows, feat), BF), DMA],
    )
    (weight_part,) = call(weight_near, [like((feat, feat), F32)], [VM] * 3, unit, pack, mean_own, feat_own)
    (back,) = call(
        back_far,
        [like((chips, width + 2 * deep + share, feat))],
        [VM] * 7,
        5 * unit,
        pack_far,
        weight_neigh,
        degree_far,
        ship_far,
        hub_part,
        cut_part,
        weight_part,
        to=[HB],
        scratch=[
            pltpu.VMEM((chips, width, feat), BF),
            pltpu.VMEM((chips, 2 * deep, feat), BF),
            pltpu.VMEM((chips, share, feat), BF),
            DMA((3,)),
        ],
    )
    back = over_chips(back)
    (row_sum,) = call(
        row_terms, [like((rows, feat), F32)], [SM] + [VM] * 4, 3 * unit, tile_cols, pack, weight_self, local_weight, gmean
    )
    (weight_sum,) = call(
        spread,
        [like((chips, share, feat))],
        [VM],
        1 << 20,
        back,
        to=[HB],
        scratch=[pltpu.VMEM((chips, share, feat), BF), DMA],
    )
    weight_all = over_chips(weight_sum)
    weight_pair = pair(weight_all)
    (feature_grad,) = call(
        finish,
        [like((rows, feat))],
        [SM] + [VM] * 4,
        2 * unit,
        row_counts,
        row_sum,
        routes,
        hub_ids,
        back,
    )
    grads = [like((feat, feat), F32)] * 2
    held = [pltpu.VMEM((2, half, feat), F32), DMA((2,))]
    halfway = call(place_own, grads, [SM, VM], 1 << 20, core, weight_all, to=[HB, HB], scratch=held)
    grad_self, grad_neigh = call(
        place_far,
        grads,
        [SM, VM, HB, HB],
        1 << 20,
        core,
        weight_pair,
        *halfway,
        to=[HB, HB],
        scratch=held,
        alias={2: 0, 3: 1},
    )
    return activated, feature_grad, grad_self, grad_neigh


def solution(mesh):
    finer = Mesh(mesh.devices.reshape(4, 4, 4, 2), DOM)
    in_specs = (
        P(DOM, None),
        P(),
        P(),
        P(DOM, None),
        P(DOM, None),
        P(DOM, None),
        P(DOM, None),
        P(None, DOM),
        P(DOM),
        P(DOM, None),
        P(DOM, None),
        P(DOM),
        P(DOM, None),
    )
    out_specs = (P(DOM, None), P(DOM, None), P(), P())

    return jax.shard_map(
        per_device, mesh=finer, in_specs=in_specs, out_specs=out_specs, check_vma=False
    )
```

```python
import jax
import jax.numpy as jnp
from jax import lax
from jax.experimental import pallas as pl
from jax.experimental.pallas import tpu as pltpu
from jax.sharding import Mesh
from jax.sharding import PartitionSpec as P


TILE = 128
TPR = 4
DOM = ("dom_0", "dom_1", "dom_2", "dom_3")
CHIPS = DOM[:3]
CORE = "dom_3"
BF = jnp.bfloat16
F32 = jnp.float32
REACH = 256


VM = pl.BlockSpec(memory_space=pltpu.VMEM)
SM = pl.BlockSpec(memory_space=pltpu.SMEM)
HB = pl.BlockSpec(memory_space=pltpu.MemorySpace.HBM)
DMA = pltpu.SemaphoreType.DMA
LIMIT = 8 << 20


def call(body, outs, specs, flops, *args, scratch=(), to=None, alias=None):
    size = sum(a.size * a.dtype.itemsize for a in args)
    size += sum(o.size * o.dtype.itemsize for o in outs)
    spaces = to or [VM] * len(outs)
    return pl.pallas_call(
        body,
        out_shape=tuple(
            pltpu.MemorySpace.HBM(o.shape, o.dtype) if p is HB else o for o, p in zip(outs, spaces)
        ),
        in_specs=list(specs),
        out_specs=tuple(spaces),
        scratch_shapes=list(scratch),
        input_output_aliases=alias or {},
        compiler_params=pltpu.CompilerParams(vmem_limit_bytes=LIMIT),
        cost_estimate=pl.CostEstimate(flops=flops, bytes_accessed=size, transcendentals=0),
    )(*args)


def mm(a, b):
    return jnp.dot(a, b, preferred_element_type=F32)


def mm_nt(a, b):
    return lax.dot_general(a, b, (((1,), (1,)), ((), ())), preferred_element_type=F32)


def mm_tn(a, b):
    return lax.dot_general(a, b, (((0,), (0,)), ((), ())), preferred_element_type=F32)


def pair(x):
    return lax.ppermute(x, CORE, [(0, 1), (1, 0)])


def round_ring(x, axis):
    size = lax.axis_size(axis)
    return [
        lax.ppermute(x, axis, [(i, (i + shift) % size) for i in range(size)])
        for shift in range(1, size)
    ]


def over_chips(x):
    return lax.all_to_all(x, CHIPS, 0, 0, tiled=True)


def iota(shape, dim):
    return lax.broadcasted_iota(jnp.int32, shape, dim)


def ones_where(cond):
    return jnp.where(cond, 1.0, 0.0).astype(BF)


def small(ids):
    return ids.astype(F32).astype(BF)


def across(table, width):
    deep, peers = table.shape
    fan = ones_where(iota((peers, width), 0) == iota((peers, width), 1) // deep)
    wide = mm(small(table), fan)
    keep = iota((deep, width), 0) == iota((deep, width), 1) % deep
    return jnp.sum(jnp.where(keep, wide, 0.0), axis=0, keepdims=True)


def send(routes_at, hub_ids_at, feats_at, out, routes, hub_ids, feats, hubs_out, cuts_out, sem):
    reads = [
        pltpu.make_async_copy(routes_at, routes, sem.at[0]),
        pltpu.make_async_copy(hub_ids_at, hub_ids, sem.at[1]),
        pltpu.make_async_copy(feats_at.at[pl.ds(0, REACH)], feats, sem.at[2]),
    ]
    for read in reads:
        read.start()
    for read in reads:
        read.wait()
    deep, peers = routes.shape
    slots = deep * peers
    width = hub_ids.shape[1]
    same = iota((width, width), 0) == iota((width, width), 1)
    hub = jnp.sum(jnp.where(same, hub_ids[...].astype(F32), 0.0), axis=1, keepdims=True)
    slab = mm(ones_where(hub.astype(jnp.int32) == iota((width, REACH), 1)), feats[...])
    hubs_out[...] = jnp.broadcast_to(slab.astype(BF)[None], hubs_out.shape)
    first = pltpu.make_async_copy(hubs_out, out.at[:, pl.ds(0, width), :], sem.at[3])
    first.start()
    fan = ones_where(iota((slots, peers), 1) == iota((slots, peers), 0) // deep)
    wide = mm_nt(fan, small(routes[...]))
    keep = iota((slots, deep), 1) == iota((slots, deep), 0) % deep
    row = jnp.sum(jnp.where(keep, wide, 0.0), axis=1, keepdims=True).astype(jnp.int32)
    rows = mm(ones_where(row == iota((slots, REACH), 1)), feats[...])
    cuts_out[...] = rows.astype(BF).reshape(cuts_out.shape)
    second = pltpu.make_async_copy(
        cuts_out, out.at[:, pl.ds(width, cuts_out.shape[1]), :], sem.at[4]
    )
    second.start()
    first.wait()
    second.wait()


def ahead(
    cols,
    count,
    core,
    feats,
    lweight,
    cweight,
    counts,
    edges,
    hubw,
    wself,
    local_sum,
    self_term,
    degree,
    dense,
    dense_far,
    flip_own,
    cut_own,
    wide_own,
    wide_far,
    feat_own,
    ship,
    masked,
    picked,
):
    rows, feat = feats.shape
    slots = cweight.shape[1]
    hubs = 2 * dense.shape[1]
    blocks = rows // TILE
    live = count[0]
    me = core[0] % 2
    masked[...] = jnp.where(iota((rows, feat), 0) < live, feats[...], jnp.zeros_like(feats))
    self_term[...] = mm(masked[...], wself[...])
    deep = slots // counts.shape[1]
    fan = ones_where(iota((counts.shape[1], slots), 0) == iota((counts.shape[1], slots), 1) // deep)
    used = mm(small(counts[...]), fan)
    on = (iota((1, slots), 1) % deep).astype(F32) < used
    cut = cweight[...] * jnp.broadcast_to(ones_where(on), (rows, slots))
    edge_w = hubw[...]
    hub_deg = mm_tn(edge_w, jnp.ones((edge_w.shape[0], TILE), BF))[:, :1]
    degree[...] = hub_deg + jnp.sum(cut.astype(F32), axis=1, keepdims=True)
    lane = iota((TILE, TILE), 1)
    for r in range(blocks):
        part = jnp.zeros((TILE, 1), F32)
        at = pl.ds(r * TILE, TILE)
        for t in range(TPR):
            base = cols[r, t] * TILE
            picked[pl.ds(t * TILE, TILE), :] = masked[pl.ds(pl.multiple_of(base, TILE), TILE), :]
            vals = lweight[at, pl.ds(t * TILE, TILE)].astype(F32)
            part = part + jnp.sum(jnp.where(lane + base < live, vals, 0.0), axis=1, keepdims=True)
        local_sum[at, :] = mm(lweight[at, :], picked[...])
        degree[at, :] += part
    flip = jnp.transpose(cut)
    side = (iota((slots, rows), 0) // deep) % 2
    kept = jnp.where(side == me, flip, jnp.zeros_like(flip))
    tall = flip.astype(F32)
    up = pltpu.roll(tall, slots - deep, 0)
    down = pltpu.roll(tall, deep, 0)
    moved = jnp.where(side == me, jnp.where(me == 0, up, down), 0.0).astype(BF)
    cut_own[...] = kept
    wide_own[...] = jnp.transpose(kept)
    wide_far[...] = jnp.transpose(moved)
    half = feat // 2
    ship[hubs // 2 : hubs // 2 + slots, :] = moved
    feat_own[...] = jnp.transpose(jnp.where(me == 0, feats[:, :half], feats[:, half:]))
    ship[hubs // 2 + slots :, :] = jnp.transpose(
        jnp.where(me == 0, feats[:, half:], feats[:, :half])
    )
    width = hubs // (2 * (slots // (2 * deep)))
    owner = edges[...] // width
    place = ((owner % 2) ^ me) * (hubs // 2) + (owner // 2) * width + edges[...] % width
    weight = edge_w.astype(F32)
    step = 128

    def build(i, carry):
        base = pl.multiple_of(i * step, step)
        hub = iota((step, rows), 0) + base
        acc = jnp.zeros((step, rows), F32)
        for k in range(edges.shape[0]):
            acc = acc + jnp.where(place[k : k + 1, :] == hub, weight[k : k + 1, :], 0.0)
        flat = acc.astype(BF)

        @pl.when(base < hubs // 2)
        def _():
            flip_own[pl.ds(base, step), :] = flat
            dense[:, pl.ds(base, step)] = jnp.transpose(flat)

        @pl.when(base >= hubs // 2)
        def _():
            spot = pl.multiple_of(base - hubs // 2, step)
            ship[pl.ds(spot, step), :] = flat
            dense_far[:, pl.ds(spot, step)] = jnp.transpose(flat)

        return carry

    lax.fori_loop(0, hubs // step, build, 0)


def sides(bundle, width, feat):
    peers, deep, _ = bundle.shape
    table = bundle[:, :width, :].reshape(peers * width, feat)
    return table, bundle[:, width:, :].reshape(peers * (deep - width), feat)


def near_sum(wide_own, dense, bundle, out):
    _, feat = out.shape
    table, cut = sides(bundle, dense.shape[1] // bundle.shape[0], feat)
    out[...] = mm(wide_own[...], cut) + mm(dense[...], table)


def forward(
    core, count, near, local_sum, wide_far, dense, bundle, degree, self_term, wneigh, cot, act, mean_own, pack
):
    rows, feat = near.shape
    half = feat // 2
    me = core[0] % 2
    table, cut = sides(bundle, dense.shape[1] // bundle.shape[0], feat)
    total = local_sum[...] + near[...] + mm(wide_far[...], cut) + mm(dense[...], table)
    mean = (total / degree[...]).astype(BF)
    mean_own[...] = jnp.transpose(jnp.where(me == 0, mean[:, :half], mean[:, half:]))
    pack[:half, :] = jnp.transpose(jnp.where(me == 0, mean[:, half:], mean[:, :half]))
    live = iota((rows, feat), 0) < count[0]
    pre = self_term[...] + mm(mean, wneigh[...])
    sig = jax.nn.sigmoid(pre)
    act[...] = jnp.where(live, pre * sig, 0.0).astype(BF)
    grad = cot[...].astype(F32) * sig * (1.0 + pre * (1.0 - sig))
    pack[half:, :] = jnp.where(live, grad, 0.0).astype(BF)


def back_near(pack, wneigh, degree, flip_own, cut_own, gmean, hub, cut, near, sem):
    half = wneigh.shape[0] // 2
    near[...] = (mm_nt(pack[half:, :], wneigh[...]) / degree[...]).astype(BF)
    away = pltpu.make_async_copy(near, gmean, sem)
    away.start()
    hub[...] = mm(flip_own[...], near[...])
    cut[...] = mm(cut_own[...], near[...])
    away.wait()


def weight_terms(pack, pack_far, mean_own, feat_own, ship, out, terms, sem):
    half, _ = feat_own.shape
    start = ship.shape[0] - half
    peers, share, feat = out.shape
    mine, other = pack[half:, :], pack_far[half:, :]
    low = mm(feat_own[...], mine) + mm(ship[start:, :], other)
    terms[: peers // 2] = low.astype(BF).reshape(peers // 2, share, feat)
    high = mm(mean_own[...], mine) + mm(pack_far[:half, :], other)
    terms[peers // 2 :] = high.astype(BF).reshape(peers // 2, share, feat)
    away = pltpu.make_async_copy(terms, out, sem)
    away.start()
    away.wait()


def back_far(pack, wneigh, degree, ship, hub, cut, out, hubs_out, cuts_out, sem):
    feat = wneigh.shape[0]
    hubs, slots = hub.shape[0], cut.shape[0]
    width, deep = hubs_out.shape[1], cuts_out.shape[1]
    far = (mm_nt(pack[feat // 2 :, :], wneigh[...]) / degree[...]).astype(BF)
    first = hub[...] + mm(ship[:hubs, :], far)
    hubs_out[...] = first.astype(BF).reshape(hubs_out.shape)
    one = pltpu.make_async_copy(hubs_out, out.at[:, pl.ds(0, width), :], sem.at[0])
    one.start()
    second = cut[...] + mm(ship[hubs : hubs + slots, :], far)
    cuts_out[...] = second.astype(BF).reshape(cuts_out.shape)
    two = pltpu.make_async_copy(cuts_out, out.at[:, pl.ds(width, deep), :], sem.at[1])
    two.start()
    one.wait()
    two.wait()


def row_terms(cols, pack, wself, lweight, gmean, out):
    rows, feat = out.shape
    out[...] = mm_nt(pack[feat // 2 :, :], wself[...])
    for r in range(rows // TILE):
        at = pl.ds(r * TILE, TILE)
        part = mm_tn(lweight[at, :], gmean[at, :])
        for t in range(TPR):
            base = pl.multiple_of(cols[r, t] * TILE, TILE)
            out[pl.ds(base, TILE), :] += part[t * TILE : (t + 1) * TILE, :]


def own_sum(parts, out):
    out[...] = jnp.sum(parts[...].astype(F32), axis=0).astype(BF)


def join_four(a, b, c, d, out):
    rows = a.shape[0]
    for i, part in enumerate((a, b, c, d)):
        out[i * rows : (i + 1) * rows, :] = part[...]


def finish(count, rows_in, routes, hub_ids, bundle, out):
    rows, feat = rows_in.shape
    deep, peers = routes.shape
    slots = deep * peers
    chips = bundle.shape[0]
    width = hub_ids.shape[1]
    hubs = chips * width
    ids = across(routes[...], slots).astype(jnp.int32)
    cut = bundle[:, width : width + slots // chips, :].reshape(slots, feat)
    top = mm(ones_where(ids == iota((REACH, slots), 0)), cut)
    fan = ones_where(iota((width, hubs), 0) == iota((width, hubs), 1) % width)
    spots = mm(small(hub_ids[...]), fan).astype(jnp.int32)
    table = bundle[:, :width, :].reshape(hubs, feat)
    top = top + mm(ones_where(spots == iota((REACH, hubs), 0)), table)
    live = iota((rows, feat), 0) < count[0]
    out[:REACH, :] = jnp.where(live[:REACH], rows_in[:REACH, :] + top, 0.0).astype(BF)
    out[REACH:, :] = jnp.where(live[REACH:], rows_in[REACH:, :], 0.0).astype(BF)


def place_rows(spot, turn, parts, first, second, held, sem):
    rows, _ = held.shape
    half = rows // 2
    size = len(parts)
    share = parts[0].shape[0] // (size * size)
    x, z, y = spot // 32, (spot // 8) % 4, (spot // 2) % 4
    for i, part in enumerate(parts):
        wide = part[...].astype(F32)
        for k in range(size):
            for j in range(size):
                chip = ((x - i + size) % size * size + (z - k + size) % size) * size + (y - j + size) % size
                at = (k * size + j) * share
                held[pl.ds(pl.multiple_of(chip * share, share), share), :] = wide[at : at + share, :]
    to = pl.ds(pl.multiple_of(turn * half, half), half)
    one = pltpu.make_async_copy(held.at[pl.ds(0, half)], first.at[to], sem.at[0])
    two = pltpu.make_async_copy(held.at[pl.ds(half, half)], second.at[to], sem.at[1])
    one.start()
    two.start()
    one.wait()
    two.wait()


def place_own(spot, a, b, c, d, first, second, held, sem):
    place_rows(spot[0], spot[0] % 2, (a, b, c, d), first, second, held, sem)


def place_far(spot, a, b, c, d, first_in, second_in, first, second, held, sem):
    place_rows(spot[0], 1 - spot[0] % 2, (a, b, c, d), first, second, held, sem)


def per_device(
    features,
    weight_self,
    weight_neigh,
    local_weight,
    tile_cols,
    cut_weight,
    send_rows,
    send_count,
    hub_rows,
    hub_edges,
    hub_weight,
    row_counts,
    cotangent,
):
    rows, feat = features.shape
    core = lax.axis_index(DOM).astype(jnp.int32).reshape(1)
    chips = lax.axis_size(CHIPS)
    deep = send_rows.shape[1]
    width = hub_rows.shape[0]
    hubs = chips * 2 * width
    slots = chips * 2 * deep
    half = feat // 2
    share = feat // chips
    unit = 2 * 512 * 512 * 512

    def like(shape, kind=BF):
        return jax.ShapeDtypeStruct(shape, kind)

    routes = send_rows.T
    hub_ids = hub_rows.reshape(1, width)
    (bundle,) = call(
        send,
        [like((chips, width + 2 * deep, feat))],
        [HB] * 3,
        unit,
        *[pltpu.with_memory_space_constraint(x, pltpu.MemorySpace.HBM) for x in (routes, hub_ids, features)],
        to=[HB],
        scratch=[
            pltpu.VMEM(routes.shape, routes.dtype),
            pltpu.VMEM(hub_ids.shape, hub_ids.dtype),
            pltpu.VMEM((REACH, feat), BF),
            pltpu.VMEM((chips, width, feat), BF),
            pltpu.VMEM((chips, 2 * deep, feat), BF),
            DMA((5,)),
        ],
    )
    bundle = over_chips(bundle)
    (
        local_sum,
        self_term,
        degree,
        dense,
        dense_far,
        flip_own,
        cut_own,
        wide_own,
        wide_far,
        feat_own,
        ship,
    ) = call(
        ahead,
        [
            like((rows, feat), F32),
            like((rows, feat), F32),
            like((rows, 1), F32),
            like((rows, hubs // 2)),
            like((rows, hubs // 2)),
            like((hubs // 2, rows)),
            like((slots, rows)),
            like((rows, slots)),
            like((rows, slots)),
            like((half, rows)),
            like((hubs // 2 + slots + half, rows)),
        ],
        [SM, SM, SM] + [VM] * 7,
        40 * unit,
        tile_cols,
        row_counts,
        core,
        features,
        local_weight,
        cut_weight,
        send_count.T,
        hub_edges.T,
        hub_weight.T,
        weight_self,
        scratch=[pltpu.VMEM((rows, feat), BF), pltpu.VMEM((TPR * TILE, feat), BF)],
    )
    degree_far = pair(degree)
    ship_far = pair(ship)

    bundle_far = pair(bundle)
    (near,) = call(near_sum, [like((rows, feat), F32)], [VM] * 3, 3 * unit, wide_own, dense, bundle)
    activated, mean_own, pack = call(
        forward,
        [like((rows, feat)), like((half, rows)), like((half + rows, feat))],
        [SM, SM] + [VM] * 9,
        4 * unit,
        core,
        row_counts,
        near,
        local_sum,
        wide_far,
        dense_far,
        bundle_far,
        degree,
        self_term,
        weight_neigh,
        cotangent,
    )
    pack_far = pair(pack)
    gmean, hub_part, cut_part = call(
        back_near,
        [like((rows, feat)), like((hubs // 2, feat), F32), like((slots, feat), F32)],
        [VM] * 5,
        4 * unit,
        pack,
        weight_neigh,
        degree,
        flip_own,
        cut_own,
        to=[HB, VM, VM],
        scratch=[pltpu.VMEM((rows, feat), BF), DMA],
    )
    (terms,) = call(
        weight_terms,
        [like((chips, share, feat))],
        [VM] * 5,
        2 * unit,
        pack,
        pack_far,
        mean_own,
        feat_own,
        ship_far,
        to=[HB],
        scratch=[pltpu.VMEM((chips, share, feat), BF), DMA],
    )
    terms = over_chips(terms)
    (back,) = call(
        back_far,
        [like((chips, width + 2 * deep, feat))],
        [VM] * 6,
        4 * unit,
        pack_far,
        weight_neigh,
        degree_far,
        ship_far,
        hub_part,
        cut_part,
        to=[HB],
        scratch=[
            pltpu.VMEM((chips, width, feat), BF),
            pltpu.VMEM((chips, 2 * deep, feat), BF),
            DMA((2,)),
        ],
    )
    back = over_chips(back)
    (row_sum,) = call(
        row_terms, [like((rows, feat), F32)], [SM] + [VM] * 4, 3 * unit, tile_cols, pack, weight_self, local_weight, gmean
    )
    (stage,) = call(own_sum, [like((share, feat))], [VM], 1 << 20, terms)
    for axis in CHIPS[:0:-1]:
        parts = [stage] + round_ring(stage, axis)
        (stage,) = call(
            join_four, [like((4 * stage.shape[0], feat))], [VM] * 4, 1 << 20, *parts
        )
    parts = [stage] + round_ring(stage, CHIPS[0])
    (feature_grad,) = call(
        finish,
        [like((rows, feat))],
        [SM] + [VM] * 4,
        2 * unit,
        row_counts,
        row_sum,
        routes,
        hub_ids,
        back,
    )
    grads = [like((feat, feat), F32)] * 2
    held = [pltpu.VMEM((feat, feat), F32), DMA((2,))]
    halfway = call(place_own, grads, [SM] + [VM] * 4, 1 << 20, core, *parts, to=[HB, HB], scratch=held)
    grad_self, grad_neigh = call(
        place_far,
        grads,
        [SM] + [VM] * 4 + [HB, HB],
        1 << 20,
        core,
        *[pair(p) for p in parts],
        *halfway,
        to=[HB, HB],
        scratch=held,
        alias={5: 0, 6: 1},
    )
    return activated, feature_grad, grad_self, grad_neigh


def solution(mesh):
    finer = Mesh(mesh.devices.reshape(4, 4, 4, 2), DOM)
    in_specs = (
        P(DOM, None),
        P(),
        P(),
        P(DOM, None),
        P(DOM, None),
        P(DOM, None),
        P(DOM, None),
        P(None, DOM),
        P(DOM),
        P(DOM, None),
        P(DOM, None),
        P(DOM),
        P(DOM, None),
    )
    out_specs = (P(DOM, None), P(DOM, None), P(), P())

    return jax.shard_map(
        per_device, mesh=finer, in_specs=in_specs, out_specs=out_specs, check_vma=False
    )
```

```python
import jax
import jax.numpy as jnp
from jax import lax
from jax.experimental import pallas as pl
from jax.experimental.pallas import tpu as pltpu
from jax.sharding import Mesh
from jax.sharding import PartitionSpec as P


TILE = 128
TPR = 4
DOM = ("dom_0", "dom_1", "dom_2", "dom_3")
CHIPS = DOM[:3]
CORE = "dom_3"
BF = jnp.bfloat16
F32 = jnp.float32
REACH = 256


VM = pl.BlockSpec(memory_space=pltpu.VMEM)
SM = pl.BlockSpec(memory_space=pltpu.SMEM)
HB = pl.BlockSpec(memory_space=pltpu.MemorySpace.HBM)
DMA = pltpu.SemaphoreType.DMA
LIMIT = 8 << 20


def call(body, outs, specs, flops, *args, scratch=(), to=None, alias=None, limit=LIMIT):
    size = sum(a.size * a.dtype.itemsize for a in args)
    size += sum(o.size * o.dtype.itemsize for o in outs)
    spaces = to or [VM] * len(outs)
    return pl.pallas_call(
        body,
        out_shape=tuple(
            pltpu.MemorySpace.HBM(o.shape, o.dtype) if p is HB else o for o, p in zip(outs, spaces)
        ),
        in_specs=list(specs),
        out_specs=tuple(spaces),
        scratch_shapes=list(scratch),
        input_output_aliases=alias or {},
        compiler_params=pltpu.CompilerParams(vmem_limit_bytes=limit),
        cost_estimate=pl.CostEstimate(flops=flops, bytes_accessed=size, transcendentals=0),
    )(*args)


def mm(a, b):
    return jnp.dot(a, b, preferred_element_type=F32)


def mm_nt(a, b):
    return lax.dot_general(a, b, (((1,), (1,)), ((), ())), preferred_element_type=F32)


def mm_tn(a, b):
    return lax.dot_general(a, b, (((0,), (0,)), ((), ())), preferred_element_type=F32)


def pair(x):
    return lax.ppermute(x, CORE, [(0, 1), (1, 0)])


def in_hbm(x):
    return pltpu.with_memory_space_constraint(x, pltpu.MemorySpace.HBM)


def over_chips(x):
    return lax.all_to_all(x, CHIPS, 0, 0, tiled=True)


def iota(shape, dim):
    return lax.broadcasted_iota(jnp.int32, shape, dim)


def ones_where(cond):
    return jnp.where(cond, 1.0, 0.0).astype(BF)


def small(ids):
    return ids.astype(F32).astype(BF)


def across(table, width):
    deep, peers = table.shape
    fan = ones_where(iota((peers, width), 0) == iota((peers, width), 1) // deep)
    wide = mm(small(table), fan)
    keep = iota((deep, width), 0) == iota((deep, width), 1) % deep
    return jnp.sum(jnp.where(keep, wide, 0.0), axis=0, keepdims=True)


def send(routes_at, hub_ids_at, feats_at, out, routes, hub_ids, feats, hubs_out, cuts_out, sem):
    reads = [
        pltpu.make_async_copy(routes_at, routes, sem.at[0]),
        pltpu.make_async_copy(hub_ids_at, hub_ids, sem.at[1]),
        pltpu.make_async_copy(feats_at.at[pl.ds(0, REACH)], feats, sem.at[2]),
    ]
    for read in reads:
        read.start()
    for read in reads:
        read.wait()
    deep, peers = routes.shape
    slots = deep * peers
    width = hub_ids.shape[1]
    same = iota((width, width), 0) == iota((width, width), 1)
    hub = jnp.sum(jnp.where(same, hub_ids[...].astype(F32), 0.0), axis=1, keepdims=True)
    slab = mm(ones_where(hub.astype(jnp.int32) == iota((width, REACH), 1)), feats[...])
    hubs_out[...] = jnp.broadcast_to(slab.astype(BF)[None], hubs_out.shape)
    first = pltpu.make_async_copy(hubs_out, out.at[:, pl.ds(0, width), :], sem.at[3])
    first.start()
    fan = ones_where(iota((slots, peers), 1) == iota((slots, peers), 0) // deep)
    wide = mm_nt(fan, small(routes[...]))
    keep = iota((slots, deep), 1) == iota((slots, deep), 0) % deep
    row = jnp.sum(jnp.where(keep, wide, 0.0), axis=1, keepdims=True).astype(jnp.int32)
    rows = mm(ones_where(row == iota((slots, REACH), 1)), feats[...])
    cuts_out[...] = rows.astype(BF).reshape(cuts_out.shape)
    second = pltpu.make_async_copy(
        cuts_out, out.at[:, pl.ds(width, cuts_out.shape[1]), :], sem.at[4]
    )
    second.start()
    first.wait()
    second.wait()


def ahead(
    cols,
    count,
    core,
    feats_at,
    lweight_at,
    cweight_at,
    wself_at,
    counts,
    edges,
    hubw,
    local_sum_at,
    self_term_at,
    dense_at,
    flip_own_at,
    cut_own_at,
    wide_own_at,
    feat_own_at,
    degree,
    ship,
    ship_wide,
    feats,
    lweight,
    cweight,
    wself,
    local_sum,
    self_term,
    dense,
    flip_own,
    cut_own,
    wide_own,
    feat_own,
    masked,
    picked,
    sem,
):
    reads = [
        pltpu.make_async_copy(src, dst, sem.at[i])
        for i, (src, dst) in enumerate(
            ((cweight_at, cweight), (feats_at, feats), (lweight_at, lweight), (wself_at, wself))
        )
    ]
    for read in reads:
        read.start()
    writes = []

    def put(src, dst):
        write = pltpu.make_async_copy(src, dst, sem.at[4 + len(writes)])
        write.start()
        writes.append(write)

    rows, feat = feats.shape
    slots = cweight.shape[1]
    hubs = 2 * flip_own.shape[0]
    blocks = rows // TILE
    live = count[0]
    me = core[0]
    edge_w = hubw[...]
    deep = slots // counts.shape[1]
    width = hubs // (2 * (slots // (2 * deep)))
    owner = edges[...] // width
    place = ((owner % 2) ^ me) * (hubs // 2) + (owner // 2) * width + edges[...] % width
    weight = edge_w.astype(F32)
    step = 128

    def build(i, carry):
        base = pl.multiple_of(i * step, step)
        hub = iota((step, rows), 0) + base
        acc = jnp.zeros((step, rows), F32)
        for k in range(edges.shape[0]):
            acc = acc + jnp.where(place[k : k + 1, :] == hub, weight[k : k + 1, :], 0.0)
        flat = acc.astype(BF)

        @pl.when(base < hubs // 2)
        def _():
            flip_own[pl.ds(base, step), :] = flat
            dense[:, pl.ds(base, step)] = jnp.transpose(flat)

        @pl.when(base >= hubs // 2)
        def _():
            spot = pl.multiple_of(base - hubs // 2, step)
            ship[pl.ds(spot, step), :] = flat
            ship_wide[:, pl.ds(spot, step)] = jnp.transpose(flat)

        return carry

    lax.fori_loop(0, hubs // step, build, 0)
    put(flip_own, flip_own_at)
    put(dense, dense_at)
    fan = ones_where(iota((counts.shape[1], slots), 0) == iota((counts.shape[1], slots), 1) // deep)
    used = mm(small(counts[...]), fan)
    on = (iota((1, slots), 1) % deep).astype(F32) < used
    reads[0].wait()
    cut = cweight[...] * jnp.broadcast_to(ones_where(on), (rows, slots))
    hub_deg = mm_tn(edge_w, jnp.ones((edge_w.shape[0], TILE), BF))[:, :1]
    degree[...] = hub_deg + jnp.sum(cut.astype(F32), axis=1, keepdims=True)
    flip = jnp.transpose(cut)
    side = (iota((slots, rows), 0) // deep) % 2
    kept = jnp.where(side == me, flip, jnp.zeros_like(flip))
    tall = flip.astype(F32)
    up = pltpu.roll(tall, slots - deep, 0)
    down = pltpu.roll(tall, deep, 0)
    moved = jnp.where(side == me, jnp.where(me == 0, up, down), 0.0).astype(BF)
    cut_own[...] = kept
    put(cut_own, cut_own_at)
    wide_own[...] = jnp.transpose(kept)
    put(wide_own, wide_own_at)
    ship[hubs // 2 : hubs // 2 + slots, :] = moved
    ship_wide[:, hubs // 2 :] = jnp.transpose(moved)
    reads[1].wait()
    half = feat // 2
    feat_own[...] = jnp.transpose(jnp.where(me == 0, feats[:, :half], feats[:, half:]))
    put(feat_own, feat_own_at)
    ship[hubs // 2 + slots :, :] = jnp.transpose(
        jnp.where(me == 0, feats[:, half:], feats[:, :half])
    )
    masked[...] = jnp.where(iota((rows, feat), 0) < live, feats[...], jnp.zeros_like(feats))
    reads[2].wait()
    lane = iota((TILE, TILE), 1)
    for r in range(blocks):
        part = jnp.zeros((TILE, 1), F32)
        at = pl.ds(r * TILE, TILE)
        for t in range(TPR):
            base = cols[r, t] * TILE
            picked[pl.ds(t * TILE, TILE), :] = masked[pl.ds(pl.multiple_of(base, TILE), TILE), :]
            vals = lweight[at, pl.ds(t * TILE, TILE)].astype(F32)
            part = part + jnp.sum(jnp.where(lane + base < live, vals, 0.0), axis=1, keepdims=True)
        local_sum[at, :] = mm(lweight[at, :], picked[...])
        degree[at, :] += part
    put(local_sum, local_sum_at)
    reads[3].wait()
    self_term[...] = mm(masked[...], wself[...])
    put(self_term, self_term_at)
    for write in writes:
        write.wait()


def sides(bundle, width, feat):
    peers, deep, _ = bundle.shape
    table = bundle[:, :width, :].reshape(peers * width, feat)
    return table, bundle[:, width:, :].reshape(peers * (deep - width), feat)


def settle(ship_in, wide_in, degree_in, ship, wide, degree):
    pass


def fetched_sum(bundle, cut_at, dense_at, cut_w, dense_w, sem):
    feat = bundle.shape[2]
    hubs = dense_w.shape[1]
    part = hubs // 2
    reads = [pltpu.make_async_copy(cut_at, cut_w, sem.at[0])]
    for i in range(2):
        span = pl.ds(i * part, part)
        reads.append(
            pltpu.make_async_copy(dense_at.at[:, span], dense_w.at[:, span], sem.at[1 + i])
        )
    for read in reads:
        read.start()
    table, cut = sides(bundle, hubs // bundle.shape[0], feat)
    reads[0].wait()
    total = mm(cut_w[...], cut)
    reads[1].wait()
    total = total + mm(dense_w[:, :part], table[:part])
    reads[2].wait()
    return total + mm(dense_w[:, part:], table[part:])


def far_sum(wide, bundle, out, cut_w, dense_w, sem):
    hubs = dense_w.shape[1]
    slots = cut_w.shape[1]
    out[...] = fetched_sum(
        bundle, wide.at[:, pl.ds(hubs, slots)], wide.at[:, pl.ds(0, hubs)], cut_w, dense_w, sem
    ).astype(BF)


def near_sum(wide_own, dense, bundle, out, cut_w, dense_w, sem):
    out[...] = fetched_sum(bundle, wide_own, dense, cut_w, dense_w, sem)


def forward(core, count, near, far, local_sum, degree, self_term, wneigh, cot, act, mean_own, pack):
    rows, feat = near.shape
    half = feat // 2
    me = core[0]
    total = local_sum[...] + near[...] + far[...].astype(F32)
    mean = (total / degree[...]).astype(BF)
    mean_own[...] = jnp.transpose(jnp.where(me == 0, mean[:, :half], mean[:, half:]))
    pack[:half, :] = jnp.transpose(jnp.where(me == 0, mean[:, half:], mean[:, :half]))
    live = iota((rows, feat), 0) < count[0]
    pre = self_term[...] + mm(mean, wneigh[...])
    sig = jax.nn.sigmoid(pre)
    act[...] = jnp.where(live, pre * sig, 0.0).astype(BF)
    grad = cot[...].astype(F32) * sig * (1.0 + pre * (1.0 - sig))
    pack[half:, :] = jnp.where(live, grad, 0.0).astype(BF)


def back_near(pack, wneigh, degree, flip_own, cut_own, gmean, hub, cut, near, sem):
    half = wneigh.shape[0] // 2
    near[...] = (mm_nt(pack[half:, :], wneigh[...]) / degree[...]).astype(BF)
    away = pltpu.make_async_copy(near, gmean, sem)
    away.start()
    hub[...] = mm(flip_own[...], near[...])
    cut[...] = mm(cut_own[...], near[...])
    away.wait()


def weight_near(pack, mean_own, feat_own, out):
    half = feat_own.shape[0]
    grad = pack[half:, :]
    out[:half, :] = mm(feat_own[...], grad)
    out[half:, :] = mm(mean_own[...], grad)


def back_far(pack, wneigh, degree, ship, hub, cut, weight, out, hubs_out, cuts_out, weights_out, sem):
    feat = wneigh.shape[0]
    half = feat // 2
    hubs, slots = hub.shape[0], cut.shape[0]
    width, deep, share = hubs_out.shape[1], cuts_out.shape[1], weights_out.shape[1]
    peers = out.shape[0]
    grad = pack[half:, :]
    far = (mm_nt(grad, wneigh[...]) / degree[...]).astype(BF)
    first = hub[...] + mm(ship[:hubs, :], far)
    hubs_out[...] = first.astype(BF).reshape(hubs_out.shape)
    one = pltpu.make_async_copy(hubs_out, out.at[:, pl.ds(0, width), :], sem.at[0])
    one.start()
    second = cut[...] + mm(ship[hubs : hubs + slots, :], far)
    cuts_out[...] = second.astype(BF).reshape(cuts_out.shape)
    two = pltpu.make_async_copy(cuts_out, out.at[:, pl.ds(width, deep), :], sem.at[1])
    two.start()
    low = weight[:half, :] + mm(ship[hubs + slots :, :], grad)
    weights_out[: peers // 2] = low.astype(BF).reshape(peers // 2, share, feat)
    high = weight[half:, :] + mm(pack[:half, :], grad)
    weights_out[peers // 2 :] = high.astype(BF).reshape(peers // 2, share, feat)
    three = pltpu.make_async_copy(weights_out, out.at[:, pl.ds(width + deep, share), :], sem.at[2])
    three.start()
    one.wait()
    two.wait()
    three.wait()


def row_terms(cols, pack, wself, lweight, gmean, out):
    rows, feat = out.shape
    out[...] = mm_nt(pack[feat // 2 :, :], wself[...])
    for r in range(rows // TILE):
        at = pl.ds(r * TILE, TILE)
        part = mm_tn(lweight[at, :], gmean[at, :])
        for t in range(TPR):
            base = pl.multiple_of(cols[r, t] * TILE, TILE)
            out[pl.ds(base, TILE), :] += part[t * TILE : (t + 1) * TILE, :]


def spread(parts, out, held, sem):
    share = held.shape[1]
    first = parts.shape[1] - share
    total = jnp.sum(parts[:, first:, :].astype(F32), axis=0)
    held[...] = jnp.broadcast_to(total.astype(BF)[None], held.shape)
    away = pltpu.make_async_copy(held, out, sem)
    away.start()
    away.wait()


def finish(count, rows_in, routes, hub_ids, bundle, out):
    rows, feat = rows_in.shape
    deep, peers = routes.shape
    slots = deep * peers
    chips = bundle.shape[0]
    width = hub_ids.shape[1]
    hubs = chips * width
    ids = across(routes[...], slots).astype(jnp.int32)
    cut = bundle[:, width : width + slots // chips, :].reshape(slots, feat)
    top = mm(ones_where(ids == iota((REACH, slots), 0)), cut)
    fan = ones_where(iota((width, hubs), 0) == iota((width, hubs), 1) % width)
    spots = mm(small(hub_ids[...]), fan).astype(jnp.int32)
    table = bundle[:, :width, :].reshape(hubs, feat)
    top = top + mm(ones_where(spots == iota((REACH, hubs), 0)), table)
    live = iota((rows, feat), 0) < count[0]
    out[:REACH, :] = jnp.where(live[:REACH], rows_in[:REACH, :] + top, 0.0).astype(BF)
    out[REACH:, :] = jnp.where(live[REACH:], rows_in[REACH:, :], 0.0).astype(BF)


def place_rows(turn, source, first, second, held, sem):
    half, feat = held.shape[1:]
    whole = source[...].reshape(2 * half, feat).astype(F32)
    at = pl.ds(pl.multiple_of(turn * half, half), half)
    held[0] = whole[:half, :]
    one = pltpu.make_async_copy(held.at[0], first.at[at], sem.at[0])
    one.start()
    held[1] = whole[half:, :]
    two = pltpu.make_async_copy(held.at[1], second.at[at], sem.at[1])
    two.start()
    one.wait()
    two.wait()


def place_own(core, source, first, second, held, sem):
    place_rows(core[0], source, first, second, held, sem)


def place_far(core, source, first_in, second_in, first, second, held, sem):
    place_rows(1 - core[0], source, first, second, held, sem)


def per_device(
    features,
    weight_self,
    weight_neigh,
    local_weight,
    tile_cols,
    cut_weight,
    send_rows,
    send_count,
    hub_rows,
    hub_edges,
    hub_weight,
    row_counts,
    cotangent,
):
    rows, feat = features.shape
    core = lax.axis_index(CORE).astype(jnp.int32).reshape(1)
    chips = lax.axis_size(CHIPS)
    deep = send_rows.shape[1]
    width = hub_rows.shape[0]
    hubs = chips * 2 * width
    slots = chips * 2 * deep
    half = feat // 2
    share = feat // chips
    unit = 2 * 512 * 512 * 512

    def like(shape, kind=BF):
        return jax.ShapeDtypeStruct(shape, kind)

    routes = send_rows.T
    hub_ids = hub_rows.reshape(1, width)
    (bundle,) = call(
        send,
        [like((chips, width + 2 * deep, feat))],
        [HB] * 3,
        unit,
        *[in_hbm(x) for x in (routes, hub_ids, features)],
        to=[HB],
        scratch=[
            pltpu.VMEM(routes.shape, routes.dtype),
            pltpu.VMEM(hub_ids.shape, hub_ids.dtype),
            pltpu.VMEM((REACH, feat), BF),
            pltpu.VMEM((chips, width, feat), BF),
            pltpu.VMEM((chips, 2 * deep, feat), BF),
            DMA((5,)),
        ],
    )
    bundle = over_chips(bundle)
    held = [
        like((rows, feat), F32),
        like((rows, feat), F32),
        like((rows, hubs // 2)),
        like((hubs // 2, rows)),
        like((slots, rows)),
        like((rows, slots)),
        like((half, rows)),
    ]
    sources = (features, local_weight, cut_weight, weight_self)
    local_sum, self_term, dense, flip_own, cut_own, wide_own, feat_own, degree, ship, ship_wide = call(
        ahead,
        held
        + [
            like((rows, 1), F32),
            like((hubs // 2 + slots + half, rows)),
            like((rows, hubs // 2 + slots)),
        ],
        [SM, SM, SM] + [HB] * 4 + [VM] * 3,
        40 * unit,
        tile_cols,
        row_counts,
        core,
        *[in_hbm(x) for x in sources],
        send_count.T,
        hub_edges.T,
        hub_weight.T,
        to=[HB] * len(held) + [VM] * 3,
        scratch=[pltpu.VMEM(x.shape, x.dtype) for x in (*sources, *held)]
        + [pltpu.VMEM((rows, feat), BF), pltpu.VMEM((TPR * TILE, feat), BF), DMA((4 + len(held),))],
        limit=20 << 20,
    )
    pairs = [in_hbm(pair(x)) for x in (ship, ship_wide, degree)]
    ship_far, wide_far, degree_far = call(
        settle,
        [like(x.shape, x.dtype) for x in (ship, ship_wide, degree)],
        [HB] * 3,
        1 << 20,
        *pairs,
        to=[HB] * 3,
        alias={0: 0, 1: 1, 2: 2},
    )
    weights = [pltpu.VMEM((rows, slots), BF), pltpu.VMEM((rows, hubs // 2), BF), DMA((3,))]
    (far,) = call(
        far_sum, [like((rows, feat))], [HB, VM], 3 * unit, in_hbm(wide_far), bundle, scratch=weights
    )
    far = pair(far)
    (near,) = call(
        near_sum,
        [like((rows, feat), F32)],
        [HB, HB, VM],
        3 * unit,
        in_hbm(wide_own),
        in_hbm(dense),
        bundle,
        scratch=weights,
    )
    activated, mean_own, pack = call(
        forward,
        [like((rows, feat)), like((half, rows)), like((half + rows, feat))],
        [SM, SM] + [VM] * 7,
        unit,
        core,
        row_counts,
        near,
        far,
        local_sum,
        degree,
        self_term,
        weight_neigh,
        cotangent,
    )
    pack_far = pair(pack)
    gmean, hub_part, cut_part = call(
        back_near,
        [like((rows, feat)), like((hubs // 2, feat), F32), like((slots, feat), F32)],
        [VM] * 5,
        4 * unit,
        pack,
        weight_neigh,
        degree,
        flip_own,
        cut_own,
        to=[HB, VM, VM],
        scratch=[pltpu.VMEM((rows, feat), BF), DMA],
    )
    (weight_part,) = call(weight_near, [like((feat, feat), F32)], [VM] * 3, unit, pack, mean_own, feat_own)
    (back,) = call(
        back_far,
        [like((chips, width + 2 * deep + share, feat))],
        [VM] * 7,
        5 * unit,
        pack_far,
        weight_neigh,
        degree_far,
        ship_far,
        hub_part,
        cut_part,
        weight_part,
        to=[HB],
        scratch=[
            pltpu.VMEM((chips, width, feat), BF),
            pltpu.VMEM((chips, 2 * deep, feat), BF),
            pltpu.VMEM((chips, share, feat), BF),
            DMA((3,)),
        ],
    )
    back = over_chips(back)
    (row_sum,) = call(
        row_terms, [like((rows, feat), F32)], [SM] + [VM] * 4, 3 * unit, tile_cols, pack, weight_self, local_weight, gmean
    )
    (weight_sum,) = call(
        spread,
        [like((chips, share, feat))],
        [VM],
        1 << 20,
        back,
        to=[HB],
        scratch=[pltpu.VMEM((chips, share, feat), BF), DMA],
    )
    weight_all = over_chips(weight_sum)
    weight_pair = pair(weight_all)
    (feature_grad,) = call(
        finish,
        [like((rows, feat))],
        [SM] + [VM] * 4,
        2 * unit,
        row_counts,
        row_sum,
        routes,
        hub_ids,
        back,
    )
    grads = [like((feat, feat), F32)] * 2
    wide = [pltpu.VMEM((2, half, feat), F32), DMA((2,))]
    halfway = call(place_own, grads, [SM, VM], 1 << 20, core, weight_all, to=[HB, HB], scratch=wide)
    grad_self, grad_neigh = call(
        place_far,
        grads,
        [SM, VM, HB, HB],
        1 << 20,
        core,
        weight_pair,
        *halfway,
        to=[HB, HB],
        scratch=wide,
        alias={2: 0, 3: 1},
    )
    return activated, feature_grad, grad_self, grad_neigh


def solution(mesh):
    finer = Mesh(mesh.devices.reshape(4, 4, 4, 2), DOM)
    in_specs = (
        P(DOM, None),
        P(),
        P(),
        P(DOM, None),
        P(DOM, None),
        P(DOM, None),
        P(DOM, None),
        P(None, DOM),
        P(DOM),
        P(DOM, None),
        P(DOM, None),
        P(DOM),
        P(DOM, None),
    )
    out_specs = (P(DOM, None), P(DOM, None), P(), P())

    return jax.shard_map(
        per_device, mesh=finer, in_specs=in_specs, out_specs=out_specs, check_vma=False
    )
```

```python
import jax
import jax.numpy as jnp
from jax import lax
from jax.experimental import pallas as pl
from jax.experimental.pallas import tpu as pltpu
from jax.sharding import Mesh
from jax.sharding import PartitionSpec as P


TILE = 128
TPR = 4
DOM = ("dom_0", "dom_1", "dom_2", "dom_3")
CHIPS = DOM[:3]
CORE = "dom_3"
BF = jnp.bfloat16
F32 = jnp.float32
REACH = 256


VM = pl.BlockSpec(memory_space=pltpu.VMEM)
SM = pl.BlockSpec(memory_space=pltpu.SMEM)
HB = pl.BlockSpec(memory_space=pltpu.MemorySpace.HBM)
DMA = pltpu.SemaphoreType.DMA
LIMIT = 8 << 20


def call(body, outs, specs, flops, *args, scratch=(), to=None, alias=None, limit=LIMIT):
    size = sum(a.size * a.dtype.itemsize for a in args)
    size += sum(o.size * o.dtype.itemsize for o in outs)
    spaces = to or [VM] * len(outs)
    return pl.pallas_call(
        body,
        out_shape=tuple(
            pltpu.MemorySpace.HBM(o.shape, o.dtype) if p is HB else o for o, p in zip(outs, spaces)
        ),
        in_specs=list(specs),
        out_specs=tuple(spaces),
        scratch_shapes=list(scratch),
        input_output_aliases=alias or {},
        compiler_params=pltpu.CompilerParams(vmem_limit_bytes=limit),
        cost_estimate=pl.CostEstimate(flops=flops, bytes_accessed=size, transcendentals=0),
    )(*args)


def mm(a, b):
    return jnp.dot(a, b, preferred_element_type=F32)


def mm_nt(a, b):
    return lax.dot_general(a, b, (((1,), (1,)), ((), ())), preferred_element_type=F32)


def mm_tn(a, b):
    return lax.dot_general(a, b, (((0,), (0,)), ((), ())), preferred_element_type=F32)


def pair(x):
    return lax.ppermute(x, CORE, [(0, 1), (1, 0)])


def in_hbm(x):
    return pltpu.with_memory_space_constraint(x, pltpu.MemorySpace.HBM)


def over_chips(x):
    return lax.all_to_all(x, CHIPS, 0, 0, tiled=True)


def iota(shape, dim):
    return lax.broadcasted_iota(jnp.int32, shape, dim)


def ones_where(cond):
    return jnp.where(cond, 1.0, 0.0).astype(BF)


def small(ids):
    return ids.astype(F32).astype(BF)


def across(table, width):
    deep, peers = table.shape
    fan = ones_where(iota((peers, width), 0) == iota((peers, width), 1) // deep)
    wide = mm(small(table), fan)
    keep = iota((deep, width), 0) == iota((deep, width), 1) % deep
    return jnp.sum(jnp.where(keep, wide, 0.0), axis=0, keepdims=True)


def send(routes_at, hub_ids_at, feats_at, out, routes, hub_ids, feats, hubs_out, cuts_out, sem):
    reads = [
        pltpu.make_async_copy(routes_at, routes, sem.at[0]),
        pltpu.make_async_copy(hub_ids_at, hub_ids, sem.at[1]),
        pltpu.make_async_copy(feats_at.at[pl.ds(0, REACH)], feats, sem.at[2]),
    ]
    for read in reads:
        read.start()
    for read in reads:
        read.wait()
    deep, peers = routes.shape
    slots = deep * peers
    width = hub_ids.shape[1]
    same = iota((width, width), 0) == iota((width, width), 1)
    hub = jnp.sum(jnp.where(same, hub_ids[...].astype(F32), 0.0), axis=1, keepdims=True)
    slab = mm(ones_where(hub.astype(jnp.int32) == iota((width, REACH), 1)), feats[...])
    hubs_out[...] = jnp.broadcast_to(slab.astype(BF)[None], hubs_out.shape)
    first = pltpu.make_async_copy(hubs_out, out.at[:, pl.ds(0, width), :], sem.at[3])
    first.start()
    fan = ones_where(iota((slots, peers), 1) == iota((slots, peers), 0) // deep)
    wide = mm_nt(fan, small(routes[...]))
    keep = iota((slots, deep), 1) == iota((slots, deep), 0) % deep
    row = jnp.sum(jnp.where(keep, wide, 0.0), axis=1, keepdims=True).astype(jnp.int32)
    rows = mm(ones_where(row == iota((slots, REACH), 1)), feats[...])
    cuts_out[...] = rows.astype(BF).reshape(cuts_out.shape)
    second = pltpu.make_async_copy(
        cuts_out, out.at[:, pl.ds(width, cuts_out.shape[1]), :], sem.at[4]
    )
    second.start()
    first.wait()
    second.wait()


def ahead(
    cols,
    count,
    core,
    feats_at,
    lweight_at,
    cweight_at,
    wself_at,
    counts,
    edges,
    hubw,
    local_sum_at,
    self_term_at,
    dense_at,
    flip_own_at,
    cut_own_at,
    wide_own_at,
    feat_own_at,
    dense_far_at,
    wide_far_at,
    degree_at,
    ship,
    feats,
    lweight,
    cweight,
    wself,
    local_sum,
    self_term,
    dense,
    flip_own,
    cut_own,
    wide_own,
    feat_own,
    dense_far,
    wide_far,
    degree,
    masked,
    picked,
    sem,
):
    reads = [
        pltpu.make_async_copy(src, dst, sem.at[i])
        for i, (src, dst) in enumerate(
            ((cweight_at, cweight), (feats_at, feats), (lweight_at, lweight), (wself_at, wself))
        )
    ]
    for read in reads:
        read.start()
    writes = []

    def put(src, dst):
        write = pltpu.make_async_copy(src, dst, sem.at[4 + len(writes)])
        write.start()
        writes.append(write)

    rows, feat = feats.shape
    slots = cweight.shape[1]
    hubs = 2 * flip_own.shape[0]
    blocks = rows // TILE
    live = count[0]
    me = core[0]
    edge_w = hubw[...]
    deep = slots // counts.shape[1]
    width = hubs // (2 * (slots // (2 * deep)))
    owner = edges[...] // width
    place = ((owner % 2) ^ me) * (hubs // 2) + (owner // 2) * width + edges[...] % width
    weight = edge_w.astype(F32)
    step = 128

    def build(i, carry):
        base = pl.multiple_of(i * step, step)
        hub = iota((step, rows), 0) + base
        acc = jnp.zeros((step, rows), F32)
        for k in range(edges.shape[0]):
            acc = acc + jnp.where(place[k : k + 1, :] == hub, weight[k : k + 1, :], 0.0)
        flat = acc.astype(BF)

        @pl.when(base < hubs // 2)
        def _():
            flip_own[pl.ds(base, step), :] = flat
            dense[:, pl.ds(base, step)] = jnp.transpose(flat)

        @pl.when(base >= hubs // 2)
        def _():
            spot = pl.multiple_of(base - hubs // 2, step)
            ship[pl.ds(spot, step), :] = flat
            dense_far[:, pl.ds(spot, step)] = jnp.transpose(flat)

        return carry

    lax.fori_loop(0, hubs // step, build, 0)
    put(flip_own, flip_own_at)
    put(dense, dense_at)
    put(dense_far, dense_far_at)
    fan = ones_where(iota((counts.shape[1], slots), 0) == iota((counts.shape[1], slots), 1) // deep)
    used = mm(small(counts[...]), fan)
    on = (iota((1, slots), 1) % deep).astype(F32) < used
    reads[0].wait()
    cut = cweight[...] * jnp.broadcast_to(ones_where(on), (rows, slots))
    hub_deg = mm_tn(edge_w, jnp.ones((edge_w.shape[0], TILE), BF))[:, :1]
    degree[...] = hub_deg + jnp.sum(cut.astype(F32), axis=1, keepdims=True)
    flip = jnp.transpose(cut)
    side = (iota((slots, rows), 0) // deep) % 2
    kept = jnp.where(side == me, flip, jnp.zeros_like(flip))
    tall = flip.astype(F32)
    up = pltpu.roll(tall, slots - deep, 0)
    down = pltpu.roll(tall, deep, 0)
    moved = jnp.where(side == me, jnp.where(me == 0, up, down), 0.0).astype(BF)
    cut_own[...] = kept
    put(cut_own, cut_own_at)
    wide_own[...] = jnp.transpose(kept)
    put(wide_own, wide_own_at)
    ship[hubs // 2 : hubs // 2 + slots, :] = moved
    wide_far[...] = jnp.transpose(moved)
    put(wide_far, wide_far_at)
    reads[1].wait()
    half = feat // 2
    feat_own[...] = jnp.transpose(jnp.where(me == 0, feats[:, :half], feats[:, half:]))
    put(feat_own, feat_own_at)
    ship[hubs // 2 + slots :, :] = jnp.transpose(
        jnp.where(me == 0, feats[:, half:], feats[:, :half])
    )
    masked[...] = jnp.where(iota((rows, feat), 0) < live, feats[...], jnp.zeros_like(feats))
    reads[2].wait()
    lane = iota((TILE, TILE), 1)
    for r in range(blocks):
        part = jnp.zeros((TILE, 1), F32)
        at = pl.ds(r * TILE, TILE)
        for t in range(TPR):
            base = cols[r, t] * TILE
            picked[pl.ds(t * TILE, TILE), :] = masked[pl.ds(pl.multiple_of(base, TILE), TILE), :]
            vals = lweight[at, pl.ds(t * TILE, TILE)].astype(F32)
            part = part + jnp.sum(jnp.where(lane + base < live, vals, 0.0), axis=1, keepdims=True)
        local_sum[at, :] = mm(lweight[at, :], picked[...])
        degree[at, :] += part
    put(local_sum, local_sum_at)
    put(degree, degree_at)
    reads[3].wait()
    self_term[...] = mm(masked[...], wself[...])
    put(self_term, self_term_at)
    for write in writes:
        write.wait()


def sides(bundle, width, feat):
    peers, deep, _ = bundle.shape
    table = bundle[:, :width, :].reshape(peers * width, feat)
    return table, bundle[:, width:, :].reshape(peers * (deep - width), feat)


def settle(ship_in, degree_in, ship, degree):
    pass


def near_sum(
    wide_at,
    dense_at,
    local_at,
    dense_far_at,
    wide_far_at,
    self_at,
    degree_at,
    cot_at,
    wneigh_at,
    bundle,
    out,
    dense_far,
    wide_far,
    self_term,
    degree,
    cot,
    wneigh,
    wide,
    dense,
    local,
    sem,
):
    pairs = (
        (wide_at, wide),
        (dense_at, dense),
        (local_at, local),
        (wide_far_at, wide_far),
        (dense_far_at, dense_far),
        (self_at, self_term),
        (degree_at, degree),
        (wneigh_at, wneigh),
        (cot_at, cot),
    )
    reads = [pltpu.make_async_copy(src, dst, sem.at[i]) for i, (src, dst) in enumerate(pairs)]
    for read in reads:
        read.start()
    _, feat = out.shape
    table, cut = sides(bundle, dense.shape[1] // bundle.shape[0], feat)
    reads[0].wait()
    total = mm(wide[...], cut)
    reads[1].wait()
    total = total + mm(dense[...], table)
    reads[2].wait()
    out[...] = total + local[...]
    for read in reads[3:]:
        read.wait()


def forward(
    core,
    count,
    flip_at,
    cut_at,
    feat_at,
    ship_at,
    degree_far_at,
    near,
    wide_far,
    dense,
    bundle,
    degree,
    self_term,
    wneigh,
    cot,
    act_at,
    mean_own,
    pack,
    flip,
    cut_own,
    feat_own,
    ship,
    degree_far,
    act,
    sem,
):
    pairs = (
        (flip_at, flip),
        (cut_at, cut_own),
        (feat_at, feat_own),
        (ship_at, ship),
        (degree_far_at, degree_far),
    )
    reads = [pltpu.make_async_copy(src, dst, sem.at[i]) for i, (src, dst) in enumerate(pairs)]
    for read in reads:
        read.start()
    rows, feat = near.shape
    half = feat // 2
    me = core[0]
    table, cut = sides(bundle, dense.shape[1] // bundle.shape[0], feat)
    total = near[...] + mm(wide_far[...], cut) + mm(dense[...], table)
    mean = (total / degree[...]).astype(BF)
    mean_own[...] = jnp.transpose(jnp.where(me == 0, mean[:, :half], mean[:, half:]))
    pack[:half, :] = jnp.transpose(jnp.where(me == 0, mean[:, half:], mean[:, :half]))
    live = iota((rows, feat), 0) < count[0]
    pre = self_term[...] + mm(mean, wneigh[...])
    sig = jax.nn.sigmoid(pre)
    act[...] = jnp.where(live, pre * sig, 0.0).astype(BF)
    away = pltpu.make_async_copy(act, act_at, sem.at[len(reads)])
    away.start()
    grad = cot[...].astype(F32) * sig * (1.0 + pre * (1.0 - sig))
    pack[half:, :] = jnp.where(live, grad, 0.0).astype(BF)
    for read in reads:
        read.wait()
    away.wait()


def back_near(pack, wneigh, degree, flip_own, cut_own, gmean, hub, cut, near, sem):
    half = wneigh.shape[0] // 2
    near[...] = (mm_nt(pack[half:, :], wneigh[...]) / degree[...]).astype(BF)
    away = pltpu.make_async_copy(near, gmean, sem)
    away.start()
    hub[...] = mm(flip_own[...], near[...])
    cut[...] = mm(cut_own[...], near[...])
    away.wait()


def weight_near(pack, mean_own, feat_own, out):
    half = feat_own.shape[0]
    grad = pack[half:, :]
    out[:half, :] = mm(feat_own[...], grad)
    out[half:, :] = mm(mean_own[...], grad)


def back_far(pack, wneigh, degree, ship, hub, cut, weight, out, hubs_out, cuts_out, weights_out, sem):
    feat = wneigh.shape[0]
    half = feat // 2
    hubs, slots = hub.shape[0], cut.shape[0]
    width, deep, share = hubs_out.shape[1], cuts_out.shape[1], weights_out.shape[1]
    peers = out.shape[0]
    grad = pack[half:, :]
    far = (mm_nt(grad, wneigh[...]) / degree[...]).astype(BF)
    first = hub[...] + mm(ship[:hubs, :], far)
    hubs_out[...] = first.astype(BF).reshape(hubs_out.shape)
    one = pltpu.make_async_copy(hubs_out, out.at[:, pl.ds(0, width), :], sem.at[0])
    one.start()
    second = cut[...] + mm(ship[hubs : hubs + slots, :], far)
    cuts_out[...] = second.astype(BF).reshape(cuts_out.shape)
    two = pltpu.make_async_copy(cuts_out, out.at[:, pl.ds(width, deep), :], sem.at[1])
    two.start()
    low = weight[:half, :] + mm(ship[hubs + slots :, :], grad)
    weights_out[: peers // 2] = low.astype(BF).reshape(peers // 2, share, feat)
    high = weight[half:, :] + mm(pack[:half, :], grad)
    weights_out[peers // 2 :] = high.astype(BF).reshape(peers // 2, share, feat)
    three = pltpu.make_async_copy(weights_out, out.at[:, pl.ds(width + deep, share), :], sem.at[2])
    three.start()
    one.wait()
    two.wait()
    three.wait()


def row_terms(cols, pack, wself, lweight, gmean, out):
    rows, feat = out.shape
    out[...] = mm_nt(pack[feat // 2 :, :], wself[...])
    for r in range(rows // TILE):
        at = pl.ds(r * TILE, TILE)
        part = mm_tn(lweight[at, :], gmean[at, :])
        for t in range(TPR):
            base = pl.multiple_of(cols[r, t] * TILE, TILE)
            out[pl.ds(base, TILE), :] += part[t * TILE : (t + 1) * TILE, :]


def spread(parts, out, held, sem):
    share = held.shape[1]
    first = parts.shape[1] - share
    total = jnp.sum(parts[:, first:, :].astype(F32), axis=0)
    held[...] = jnp.broadcast_to(total.astype(BF)[None], held.shape)
    away = pltpu.make_async_copy(held, out, sem)
    away.start()
    away.wait()


def finish(count, rows_in, routes, hub_ids, bundle, out):
    rows, feat = rows_in.shape
    deep, peers = routes.shape
    slots = deep * peers
    chips = bundle.shape[0]
    width = hub_ids.shape[1]
    hubs = chips * width
    ids = across(routes[...], slots).astype(jnp.int32)
    cut = bundle[:, width : width + slots // chips, :].reshape(slots, feat)
    top = mm(ones_where(ids == iota((REACH, slots), 0)), cut)
    fan = ones_where(iota((width, hubs), 0) == iota((width, hubs), 1) % width)
    spots = mm(small(hub_ids[...]), fan).astype(jnp.int32)
    table = bundle[:, :width, :].reshape(hubs, feat)
    top = top + mm(ones_where(spots == iota((REACH, hubs), 0)), table)
    live = iota((rows, feat), 0) < count[0]
    out[:REACH, :] = jnp.where(live[:REACH], rows_in[:REACH, :] + top, 0.0).astype(BF)
    out[REACH:, :] = jnp.where(live[REACH:], rows_in[REACH:, :], 0.0).astype(BF)


def place_rows(turn, source, first, second, held, sem):
    half, feat = held.shape[1:]
    whole = source[...].reshape(2 * half, feat).astype(F32)
    at = pl.ds(pl.multiple_of(turn * half, half), half)
    held[0] = whole[:half, :]
    one = pltpu.make_async_copy(held.at[0], first.at[at], sem.at[0])
    one.start()
    held[1] = whole[half:, :]
    two = pltpu.make_async_copy(held.at[1], second.at[at], sem.at[1])
    two.start()
    one.wait()
    two.wait()


def place_own(core, source, first, second, held, sem):
    place_rows(core[0], source, first, second, held, sem)


def place_far(core, source, first_in, second_in, first, second, held, sem):
    place_rows(1 - core[0], source, first, second, held, sem)


def per_device(
    features,
    weight_self,
    weight_neigh,
    local_weight,
    tile_cols,
    cut_weight,
    send_rows,
    send_count,
    hub_rows,
    hub_edges,
    hub_weight,
    row_counts,
    cotangent,
):
    rows, feat = features.shape
    core = lax.axis_index(CORE).astype(jnp.int32).reshape(1)
    chips = lax.axis_size(CHIPS)
    deep = send_rows.shape[1]
    width = hub_rows.shape[0]
    hubs = chips * 2 * width
    slots = chips * 2 * deep
    half = feat // 2
    share = feat // chips
    unit = 2 * 512 * 512 * 512

    def like(shape, kind=BF):
        return jax.ShapeDtypeStruct(shape, kind)

    routes = send_rows.T
    hub_ids = hub_rows.reshape(1, width)
    (bundle,) = call(
        send,
        [like((chips, width + 2 * deep, feat))],
        [HB] * 3,
        unit,
        *[in_hbm(x) for x in (routes, hub_ids, features)],
        to=[HB],
        scratch=[
            pltpu.VMEM(routes.shape, routes.dtype),
            pltpu.VMEM(hub_ids.shape, hub_ids.dtype),
            pltpu.VMEM((REACH, feat), BF),
            pltpu.VMEM((chips, width, feat), BF),
            pltpu.VMEM((chips, 2 * deep, feat), BF),
            DMA((5,)),
        ],
    )
    bundle = over_chips(bundle)
    held = [
        like((rows, feat), F32),
        like((rows, feat), F32),
        like((rows, hubs // 2)),
        like((hubs // 2, rows)),
        like((slots, rows)),
        like((rows, slots)),
        like((half, rows)),
        like((rows, hubs // 2)),
        like((rows, slots)),
        like((rows, 1), F32),
    ]
    sources = (features, local_weight, cut_weight, weight_self)
    (
        local_sum,
        self_term,
        dense,
        flip_own,
        cut_own,
        wide_own,
        feat_own,
        dense_far,
        wide_far,
        degree,
        ship,
    ) = call(
        ahead,
        held + [like((hubs // 2 + slots + half, rows))],
        [SM, SM, SM] + [HB] * 4 + [VM] * 3,
        40 * unit,
        tile_cols,
        row_counts,
        core,
        *[in_hbm(x) for x in sources],
        send_count.T,
        hub_edges.T,
        hub_weight.T,
        to=[HB] * len(held) + [VM],
        scratch=[pltpu.VMEM(x.shape, x.dtype) for x in (*sources, *held)]
        + [pltpu.VMEM((rows, feat), BF), pltpu.VMEM((TPR * TILE, feat), BF), DMA((4 + len(held),))],
        limit=20 << 20,
    )
    ship_far, degree_far = call(
        settle,
        [like(ship.shape), like(degree.shape, F32)],
        [HB] * 2,
        1 << 20,
        in_hbm(pair(ship)),
        in_hbm(pair(degree)),
        to=[HB] * 2,
        alias={0: 0, 1: 1},
    )
    bundle_far = pair(bundle)
    following = [dense_far, wide_far, self_term, degree, cotangent, weight_neigh]
    near, dense_far, wide_far, self_term, degree, cotangent, weight_neigh = call(
        near_sum,
        [like((rows, feat), F32)] + [like(x.shape, x.dtype) for x in following],
        [HB] * 9 + [VM],
        3 * unit,
        *[in_hbm(x) for x in (wide_own, dense, local_sum, *following)],
        bundle,
        scratch=[pltpu.VMEM(x.shape, x.dtype) for x in (wide_own, dense, local_sum)] + [DMA((9,))],
    )
    following = [flip_own, cut_own, feat_own, ship_far, degree_far]
    activated, mean_own, pack, flip_own, cut_own, feat_own, ship_far, degree_far = call(
        forward,
        [like((rows, feat)), like((half, rows)), like((half + rows, feat))]
        + [like(x.shape, x.dtype) for x in following],
        [SM, SM] + [HB] * 5 + [VM] * 8,
        4 * unit,
        core,
        row_counts,
        *[in_hbm(x) for x in following],
        near,
        wide_far,
        dense_far,
        bundle_far,
        degree,
        self_term,
        weight_neigh,
        cotangent,
        to=[HB] + [VM] * 7,
        scratch=[pltpu.VMEM((rows, feat), BF), DMA((6,))],
    )
    pack_far = pair(pack)
    gmean, hub_part, cut_part = call(
        back_near,
        [like((rows, feat)), like((hubs // 2, feat), F32), like((slots, feat), F32)],
        [VM] * 5,
        4 * unit,
        pack,
        weight_neigh,
        degree,
        flip_own,
        cut_own,
        to=[HB, VM, VM],
        scratch=[pltpu.VMEM((rows, feat), BF), DMA],
    )
    (weight_part,) = call(weight_near, [like((feat, feat), F32)], [VM] * 3, unit, pack, mean_own, feat_own)
    (back,) = call(
        back_far,
        [like((chips, width + 2 * deep + share, feat))],
        [VM] * 7,
        5 * unit,
        pack_far,
        weight_neigh,
        degree_far,
        ship_far,
        hub_part,
        cut_part,
        weight_part,
        to=[HB],
        scratch=[
            pltpu.VMEM((chips, width, feat), BF),
            pltpu.VMEM((chips, 2 * deep, feat), BF),
            pltpu.VMEM((chips, share, feat), BF),
            DMA((3,)),
        ],
    )
    back = over_chips(back)
    (row_sum,) = call(
        row_terms, [like((rows, feat), F32)], [SM] + [VM] * 4, 3 * unit, tile_cols, pack, weight_self, local_weight, gmean
    )
    (weight_sum,) = call(
        spread,
        [like((chips, share, feat))],
        [VM],
        1 << 20,
        back,
        to=[HB],
        scratch=[pltpu.VMEM((chips, share, feat), BF), DMA],
    )
    weight_all = over_chips(weight_sum)
    weight_pair = pair(weight_all)
    (feature_grad,) = call(
        finish,
        [like((rows, feat))],
        [SM] + [VM] * 4,
        2 * unit,
        row_counts,
        row_sum,
        routes,
        hub_ids,
        back,
    )
    grads = [like((feat, feat), F32)] * 2
    wide = [pltpu.VMEM((2, half, feat), F32), DMA((2,))]
    halfway = call(place_own, grads, [SM, VM], 1 << 20, core, weight_all, to=[HB, HB], scratch=wide)
    grad_self, grad_neigh = call(
        place_far,
        grads,
        [SM, VM, HB, HB],
        1 << 20,
        core,
        weight_pair,
        *halfway,
        to=[HB, HB],
        scratch=wide,
        alias={2: 0, 3: 1},
    )
    return activated, feature_grad, grad_self, grad_neigh


def solution(mesh):
    finer = Mesh(mesh.devices.reshape(4, 4, 4, 2), DOM)
    in_specs = (
        P(DOM, None),
        P(),
        P(),
        P(DOM, None),
        P(DOM, None),
        P(DOM, None),
        P(DOM, None),
        P(None, DOM),
        P(DOM),
        P(DOM, None),
        P(DOM, None),
        P(DOM),
        P(DOM, None),
    )
    out_specs = (P(DOM, None), P(DOM, None), P(), P())

    return jax.shard_map(
        per_device, mesh=finer, in_specs=in_specs, out_specs=out_specs, check_vma=False
    )
```

```python
import jax
import jax.numpy as jnp
from jax import lax
from jax.experimental import pallas as pl
from jax.experimental.pallas import tpu as pltpu
from jax.sharding import Mesh
from jax.sharding import PartitionSpec as P


TILE = 128
TPR = 4
DOM = ("dom_0", "dom_1", "dom_2", "dom_3")
CHIPS = DOM[:3]
CORE = "dom_3"
BF = jnp.bfloat16
F32 = jnp.float32
REACH = 256


VM = pl.BlockSpec(memory_space=pltpu.VMEM)
SM = pl.BlockSpec(memory_space=pltpu.SMEM)
HB = pl.BlockSpec(memory_space=pltpu.MemorySpace.HBM)
DMA = pltpu.SemaphoreType.DMA
LIMIT = 8 << 20


def call(body, outs, specs, flops, *args, scratch=(), to=None, alias=None, limit=LIMIT):
    size = sum(a.size * a.dtype.itemsize for a in args)
    size += sum(o.size * o.dtype.itemsize for o in outs)
    spaces = to or [VM] * len(outs)
    return pl.pallas_call(
        body,
        out_shape=tuple(
            pltpu.MemorySpace.HBM(o.shape, o.dtype) if p is HB else o for o, p in zip(outs, spaces)
        ),
        in_specs=list(specs),
        out_specs=tuple(spaces),
        scratch_shapes=list(scratch),
        input_output_aliases=alias or {},
        compiler_params=pltpu.CompilerParams(vmem_limit_bytes=limit),
        cost_estimate=pl.CostEstimate(flops=flops, bytes_accessed=size, transcendentals=0),
    )(*args)


def mm(a, b):
    return jnp.dot(a, b, preferred_element_type=F32)


def mm_nt(a, b):
    return lax.dot_general(a, b, (((1,), (1,)), ((), ())), preferred_element_type=F32)


def mm_tn(a, b):
    return lax.dot_general(a, b, (((0,), (0,)), ((), ())), preferred_element_type=F32)


def pair(x):
    return lax.ppermute(x, CORE, [(0, 1), (1, 0)])


def in_hbm(x):
    return pltpu.with_memory_space_constraint(x, pltpu.MemorySpace.HBM)


def over_chips(x):
    return lax.all_to_all(x, CHIPS, 0, 0, tiled=True)


def iota(shape, dim):
    return lax.broadcasted_iota(jnp.int32, shape, dim)


def ones_where(cond):
    return jnp.where(cond, 1.0, 0.0).astype(BF)


def small(ids):
    return ids.astype(F32).astype(BF)


def across(table, width):
    deep, peers = table.shape
    fan = ones_where(iota((peers, width), 0) == iota((peers, width), 1) // deep)
    wide = mm(small(table), fan)
    keep = iota((deep, width), 0) == iota((deep, width), 1) % deep
    return jnp.sum(jnp.where(keep, wide, 0.0), axis=0, keepdims=True)


def send(routes_at, hub_ids_at, feats_at, out, routes, hub_ids, feats, hubs_out, cuts_out, sem):
    reads = [
        pltpu.make_async_copy(routes_at, routes, sem.at[0]),
        pltpu.make_async_copy(hub_ids_at, hub_ids, sem.at[1]),
        pltpu.make_async_copy(feats_at.at[pl.ds(0, REACH)], feats, sem.at[2]),
    ]
    for read in reads:
        read.start()
    for read in reads:
        read.wait()
    deep, peers = routes.shape
    slots = deep * peers
    width = hub_ids.shape[1]
    same = iota((width, width), 0) == iota((width, width), 1)
    hub = jnp.sum(jnp.where(same, hub_ids[...].astype(F32), 0.0), axis=1, keepdims=True)
    slab = mm(ones_where(hub.astype(jnp.int32) == iota((width, REACH), 1)), feats[...])
    hubs_out[...] = jnp.broadcast_to(slab.astype(BF)[None], hubs_out.shape)
    first = pltpu.make_async_copy(hubs_out, out.at[:, pl.ds(0, width), :], sem.at[3])
    first.start()
    fan = ones_where(iota((slots, peers), 1) == iota((slots, peers), 0) // deep)
    wide = mm_nt(fan, small(routes[...]))
    keep = iota((slots, deep), 1) == iota((slots, deep), 0) % deep
    row = jnp.sum(jnp.where(keep, wide, 0.0), axis=1, keepdims=True).astype(jnp.int32)
    rows = mm(ones_where(row == iota((slots, REACH), 1)), feats[...])
    cuts_out[...] = rows.astype(BF).reshape(cuts_out.shape)
    second = pltpu.make_async_copy(
        cuts_out, out.at[:, pl.ds(width, cuts_out.shape[1]), :], sem.at[4]
    )
    second.start()
    first.wait()
    second.wait()


def ahead(
    cols,
    count,
    core,
    feats_at,
    lweight_at,
    cweight_at,
    wself_at,
    counts,
    edges,
    hubw,
    local_sum_at,
    self_term_at,
    dense_at,
    flip_own_at,
    cut_own_at,
    wide_own_at,
    feat_own_at,
    dense_far_at,
    wide_far_at,
    degree_at,
    ship,
    feats,
    lweight,
    cweight,
    wself,
    local_sum,
    self_term,
    dense,
    flip_own,
    cut_own,
    wide_own,
    feat_own,
    dense_far,
    wide_far,
    degree,
    masked,
    picked,
    sem,
):
    reads = [
        pltpu.make_async_copy(src, dst, sem.at[i])
        for i, (src, dst) in enumerate(
            ((cweight_at, cweight), (feats_at, feats), (lweight_at, lweight), (wself_at, wself))
        )
    ]
    for read in reads:
        read.start()
    writes = []

    def put(src, dst):
        write = pltpu.make_async_copy(src, dst, sem.at[4 + len(writes)])
        write.start()
        writes.append(write)

    rows, feat = feats.shape
    slots = cweight.shape[1]
    hubs = 2 * flip_own.shape[0]
    blocks = rows // TILE
    live = count[0]
    me = core[0]
    edge_w = hubw[...]
    deep = slots // counts.shape[1]
    width = hubs // (2 * (slots // (2 * deep)))
    owner = edges[...] // width
    place = ((owner % 2) ^ me) * (hubs // 2) + (owner // 2) * width + edges[...] % width
    weight = edge_w.astype(F32)
    step = 128

    def build(i, carry):
        base = pl.multiple_of(i * step, step)
        hub = iota((step, rows), 0) + base
        acc = jnp.zeros((step, rows), F32)
        for k in range(edges.shape[0]):
            acc = acc + jnp.where(place[k : k + 1, :] == hub, weight[k : k + 1, :], 0.0)
        flat = acc.astype(BF)

        @pl.when(base < hubs // 2)
        def _():
            flip_own[pl.ds(base, step), :] = flat
            dense[:, pl.ds(base, step)] = jnp.transpose(flat)

        @pl.when(base >= hubs // 2)
        def _():
            spot = pl.multiple_of(base - hubs // 2, step)
            ship[pl.ds(spot, step), :] = flat
            dense_far[:, pl.ds(spot, step)] = jnp.transpose(flat)

        return carry

    lax.fori_loop(0, hubs // step, build, 0)
    put(flip_own, flip_own_at)
    put(dense, dense_at)
    put(dense_far, dense_far_at)
    fan = ones_where(iota((counts.shape[1], slots), 0) == iota((counts.shape[1], slots), 1) // deep)
    used = mm(small(counts[...]), fan)
    on = (iota((1, slots), 1) % deep).astype(F32) < used
    reads[0].wait()
    cut = cweight[...] * jnp.broadcast_to(ones_where(on), (rows, slots))
    hub_deg = mm_tn(edge_w, jnp.ones((edge_w.shape[0], TILE), BF))[:, :1]
    degree[...] = hub_deg + jnp.sum(cut.astype(F32), axis=1, keepdims=True)
    flip = jnp.transpose(cut)
    side = (iota((slots, rows), 0) // deep) % 2
    kept = jnp.where(side == me, flip, jnp.zeros_like(flip))
    tall = flip.astype(F32)
    up = pltpu.roll(tall, slots - deep, 0)
    down = pltpu.roll(tall, deep, 0)
    moved = jnp.where(side == me, jnp.where(me == 0, up, down), 0.0).astype(BF)
    cut_own[...] = kept
    put(cut_own, cut_own_at)
    wide_own[...] = jnp.transpose(kept)
    put(wide_own, wide_own_at)
    ship[hubs // 2 : hubs // 2 + slots, :] = moved
    wide_far[...] = jnp.transpose(moved)
    put(wide_far, wide_far_at)
    reads[1].wait()
    half = feat // 2
    feat_own[...] = jnp.transpose(jnp.where(me == 0, feats[:, :half], feats[:, half:]))
    put(feat_own, feat_own_at)
    ship[hubs // 2 + slots :, :] = jnp.transpose(
        jnp.where(me == 0, feats[:, half:], feats[:, :half])
    )
    masked[...] = jnp.where(iota((rows, feat), 0) < live, feats[...], jnp.zeros_like(feats))
    reads[2].wait()
    lane = iota((TILE, TILE), 1)
    for r in range(blocks):
        part = jnp.zeros((TILE, 1), F32)
        at = pl.ds(r * TILE, TILE)
        for t in range(TPR):
            base = cols[r, t] * TILE
            picked[pl.ds(t * TILE, TILE), :] = masked[pl.ds(pl.multiple_of(base, TILE), TILE), :]
            vals = lweight[at, pl.ds(t * TILE, TILE)].astype(F32)
            part = part + jnp.sum(jnp.where(lane + base < live, vals, 0.0), axis=1, keepdims=True)
        local_sum[at, :] = mm(lweight[at, :], picked[...])
        degree[at, :] += part
    put(local_sum, local_sum_at)
    put(degree, degree_at)
    reads[3].wait()
    self_term[...] = mm(masked[...], wself[...])
    put(self_term, self_term_at)
    for write in writes:
        write.wait()


def sides(bundle, width, feat):
    peers, deep, _ = bundle.shape
    table = bundle[:, :width, :].reshape(peers * width, feat)
    return table, bundle[:, width:, :].reshape(peers * (deep - width), feat)


def settle(ship_in, degree_in, ship, degree):
    pass


def near_sum(
    wide_at,
    dense_at,
    local_at,
    dense_far_at,
    wide_far_at,
    self_at,
    degree_at,
    cot_at,
    wneigh_at,
    bundle,
    out,
    dense_far,
    wide_far,
    self_term,
    degree,
    cot,
    wneigh,
    wide,
    dense,
    local,
    sem,
):
    pairs = (
        (wide_at, wide),
        (dense_at, dense),
        (local_at, local),
        (wide_far_at, wide_far),
        (dense_far_at, dense_far),
        (self_at, self_term),
        (degree_at, degree),
        (wneigh_at, wneigh),
        (cot_at, cot),
    )
    reads = [pltpu.make_async_copy(src, dst, sem.at[i]) for i, (src, dst) in enumerate(pairs)]
    for read in reads:
        read.start()
    _, feat = out.shape
    table, cut = sides(bundle, dense.shape[1] // bundle.shape[0], feat)
    reads[0].wait()
    total = mm(wide[...], cut)
    reads[1].wait()
    total = total + mm(dense[...], table)
    reads[2].wait()
    out[...] = total + local[...]
    for read in reads[3:]:
        read.wait()


def forward(
    core,
    count,
    flip_at,
    cut_at,
    feat_at,
    ship_at,
    degree_far_at,
    near,
    wide_far,
    dense,
    bundle,
    degree,
    self_term,
    wneigh,
    cot,
    act_at,
    mean_own,
    pack,
    flip,
    cut_own,
    feat_own,
    ship,
    degree_far,
    act,
    sem,
):
    pairs = (
        (flip_at, flip),
        (cut_at, cut_own),
        (feat_at, feat_own),
        (ship_at, ship),
        (degree_far_at, degree_far),
    )
    reads = [pltpu.make_async_copy(src, dst, sem.at[i]) for i, (src, dst) in enumerate(pairs)]
    for read in reads:
        read.start()
    rows, feat = near.shape
    half = feat // 2
    me = core[0]
    table, cut = sides(bundle, dense.shape[1] // bundle.shape[0], feat)
    total = near[...] + mm(wide_far[...], cut) + mm(dense[...], table)
    mean = (total / degree[...]).astype(BF)
    mean_own[...] = jnp.transpose(jnp.where(me == 0, mean[:, :half], mean[:, half:]))
    pack[:half, :] = jnp.transpose(jnp.where(me == 0, mean[:, half:], mean[:, :half]))
    live = iota((rows, feat), 0) < count[0]
    pre = self_term[...] + mm(mean, wneigh[...])
    sig = jax.nn.sigmoid(pre)
    act[...] = jnp.where(live, pre * sig, 0.0).astype(BF)
    away = pltpu.make_async_copy(act, act_at, sem.at[len(reads)])
    away.start()
    grad = cot[...].astype(F32) * sig * (1.0 + pre * (1.0 - sig))
    pack[half:, :] = jnp.where(live, grad, 0.0).astype(BF)
    for read in reads:
        read.wait()
    away.wait()


def back_near(pack, wneigh, degree, flip_own, cut_own, gmean, hub, cut, near, sem):
    half = wneigh.shape[0] // 2
    near[...] = (mm_nt(pack[half:, :], wneigh[...]) / degree[...]).astype(BF)
    away = pltpu.make_async_copy(near, gmean, sem)
    away.start()
    hub[...] = mm(flip_own[...], near[...])
    cut[...] = mm(cut_own[...], near[...])
    away.wait()


def weight_near(pack, mean_own, feat_own, out):
    half = feat_own.shape[0]
    grad = pack[half:, :]
    out[:half, :] = mm(feat_own[...], grad)
    out[half:, :] = mm(mean_own[...], grad)


def back_far(pack, wneigh, degree, ship, hub, cut, weight, out):
    feat = wneigh.shape[0]
    half = feat // 2
    hubs, slots = hub.shape[0], cut.shape[0]
    peers = out.shape[0]
    width, deep = hubs // peers, (hubs + slots) // peers
    share = out.shape[1] - deep
    grad = pack[half:, :]
    far = (mm_nt(grad, wneigh[...]) / degree[...]).astype(BF)
    low = weight[:half, :] + mm(ship[hubs + slots :, :], grad)
    out[: peers // 2, deep:, :] = low.astype(BF).reshape(peers // 2, share, feat)
    high = weight[half:, :] + mm(pack[:half, :], grad)
    out[peers // 2 :, deep:, :] = high.astype(BF).reshape(peers // 2, share, feat)
    first = hub[...] + mm(ship[:hubs, :], far)
    out[:, :width, :] = first.astype(BF).reshape(peers, width, feat)
    second = cut[...] + mm(ship[hubs : hubs + slots, :], far)
    out[:, width:deep, :] = second.astype(BF).reshape(peers, deep - width, feat)


def row_terms(cols, pack, wself, lweight, gmean, out):
    rows, feat = out.shape
    out[...] = mm_nt(pack[feat // 2 :, :], wself[...])
    for r in range(rows // TILE):
        at = pl.ds(r * TILE, TILE)
        part = mm_tn(lweight[at, :], gmean[at, :])
        for t in range(TPR):
            base = pl.multiple_of(cols[r, t] * TILE, TILE)
            out[pl.ds(base, TILE), :] += part[t * TILE : (t + 1) * TILE, :]


def spread(parts, out, held, sem):
    share = held.shape[1]
    first = parts.shape[1] - share
    total = jnp.sum(parts[:, first:, :].astype(F32), axis=0)
    held[...] = jnp.broadcast_to(total.astype(BF)[None], held.shape)
    away = pltpu.make_async_copy(held, out, sem)
    away.start()
    away.wait()


def finish(count, rows_in, routes, hub_ids, bundle, out):
    rows, feat = rows_in.shape
    deep, peers = routes.shape
    slots = deep * peers
    chips = bundle.shape[0]
    width = hub_ids.shape[1]
    hubs = chips * width
    ids = across(routes[...], slots).astype(jnp.int32)
    cut = bundle[:, width : width + slots // chips, :].reshape(slots, feat)
    top = mm(ones_where(ids == iota((REACH, slots), 0)), cut)
    fan = ones_where(iota((width, hubs), 0) == iota((width, hubs), 1) % width)
    spots = mm(small(hub_ids[...]), fan).astype(jnp.int32)
    table = bundle[:, :width, :].reshape(hubs, feat)
    top = top + mm(ones_where(spots == iota((REACH, hubs), 0)), table)
    live = iota((rows, feat), 0) < count[0]
    out[:REACH, :] = jnp.where(live[:REACH], rows_in[:REACH, :] + top, 0.0).astype(BF)
    out[REACH:, :] = jnp.where(live[REACH:], rows_in[REACH:, :], 0.0).astype(BF)


def place_rows(turn, source, first, second, held, sem):
    half, feat = held.shape[1:]
    whole = source[...].reshape(2 * half, feat).astype(F32)
    at = pl.ds(pl.multiple_of(turn * half, half), half)
    held[0] = whole[:half, :]
    one = pltpu.make_async_copy(held.at[0], first.at[at], sem.at[0])
    one.start()
    held[1] = whole[half:, :]
    two = pltpu.make_async_copy(held.at[1], second.at[at], sem.at[1])
    two.start()
    one.wait()
    two.wait()


def place_own(core, source, first, second, held, sem):
    place_rows(core[0], source, first, second, held, sem)


def place_far(core, source, first_in, second_in, first, second, held, sem):
    place_rows(1 - core[0], source, first, second, held, sem)


def per_device(
    features,
    weight_self,
    weight_neigh,
    local_weight,
    tile_cols,
    cut_weight,
    send_rows,
    send_count,
    hub_rows,
    hub_edges,
    hub_weight,
    row_counts,
    cotangent,
):
    rows, feat = features.shape
    core = lax.axis_index(CORE).astype(jnp.int32).reshape(1)
    chips = lax.axis_size(CHIPS)
    deep = send_rows.shape[1]
    width = hub_rows.shape[0]
    hubs = chips * 2 * width
    slots = chips * 2 * deep
    half = feat // 2
    share = feat // chips
    unit = 2 * 512 * 512 * 512

    def like(shape, kind=BF):
        return jax.ShapeDtypeStruct(shape, kind)

    routes = send_rows.T
    hub_ids = hub_rows.reshape(1, width)
    (bundle,) = call(
        send,
        [like((chips, width + 2 * deep, feat))],
        [HB] * 3,
        unit,
        *[in_hbm(x) for x in (routes, hub_ids, features)],
        to=[HB],
        scratch=[
            pltpu.VMEM(routes.shape, routes.dtype),
            pltpu.VMEM(hub_ids.shape, hub_ids.dtype),
            pltpu.VMEM((REACH, feat), BF),
            pltpu.VMEM((chips, width, feat), BF),
            pltpu.VMEM((chips, 2 * deep, feat), BF),
            DMA((5,)),
        ],
    )
    bundle = over_chips(bundle)
    held = [
        like((rows, feat), F32),
        like((rows, feat), F32),
        like((rows, hubs // 2)),
        like((hubs // 2, rows)),
        like((slots, rows)),
        like((rows, slots)),
        like((half, rows)),
        like((rows, hubs // 2)),
        like((rows, slots)),
        like((rows, 1), F32),
    ]
    sources = (features, local_weight, cut_weight, weight_self)
    (
        local_sum,
        self_term,
        dense,
        flip_own,
        cut_own,
        wide_own,
        feat_own,
        dense_far,
        wide_far,
        degree,
        ship,
    ) = call(
        ahead,
        held + [like((hubs // 2 + slots + half, rows))],
        [SM, SM, SM] + [HB] * 4 + [VM] * 3,
        40 * unit,
        tile_cols,
        row_counts,
        core,
        *[in_hbm(x) for x in sources],
        send_count.T,
        hub_edges.T,
        hub_weight.T,
        to=[HB] * len(held) + [VM],
        scratch=[pltpu.VMEM(x.shape, x.dtype) for x in (*sources, *held)]
        + [pltpu.VMEM((rows, feat), BF), pltpu.VMEM((TPR * TILE, feat), BF), DMA((4 + len(held),))],
        limit=20 << 20,
    )
    ship_far, degree_far = call(
        settle,
        [like(ship.shape), like(degree.shape, F32)],
        [HB] * 2,
        1 << 20,
        in_hbm(pair(ship)),
        in_hbm(pair(degree)),
        to=[HB] * 2,
        alias={0: 0, 1: 1},
    )
    bundle_far = pair(bundle)
    following = [dense_far, wide_far, self_term, degree, cotangent, weight_neigh]
    near, dense_far, wide_far, self_term, degree, cotangent, weight_neigh = call(
        near_sum,
        [like((rows, feat), F32)] + [like(x.shape, x.dtype) for x in following],
        [HB] * 9 + [VM],
        3 * unit,
        *[in_hbm(x) for x in (wide_own, dense, local_sum, *following)],
        bundle,
        scratch=[pltpu.VMEM(x.shape, x.dtype) for x in (wide_own, dense, local_sum)] + [DMA((9,))],
    )
    following = [flip_own, cut_own, feat_own, ship_far, degree_far]
    activated, mean_own, pack, flip_own, cut_own, feat_own, ship_far, degree_far = call(
        forward,
        [like((rows, feat)), like((half, rows)), like((half + rows, feat))]
        + [like(x.shape, x.dtype) for x in following],
        [SM, SM] + [HB] * 5 + [VM] * 8,
        4 * unit,
        core,
        row_counts,
        *[in_hbm(x) for x in following],
        near,
        wide_far,
        dense_far,
        bundle_far,
        degree,
        self_term,
        weight_neigh,
        cotangent,
        to=[HB] + [VM] * 7,
        scratch=[pltpu.VMEM((rows, feat), BF), DMA((6,))],
    )
    pack_far = pair(pack)
    gmean, hub_part, cut_part = call(
        back_near,
        [like((rows, feat)), like((hubs // 2, feat), F32), like((slots, feat), F32)],
        [VM] * 5,
        4 * unit,
        pack,
        weight_neigh,
        degree,
        flip_own,
        cut_own,
        to=[HB, VM, VM],
        scratch=[pltpu.VMEM((rows, feat), BF), DMA],
    )
    (weight_part,) = call(weight_near, [like((feat, feat), F32)], [VM] * 3, unit, pack, mean_own, feat_own)
    (back,) = call(
        back_far,
        [like((chips, width + 2 * deep + share, feat))],
        [VM] * 7,
        5 * unit,
        pack_far,
        weight_neigh,
        degree_far,
        ship_far,
        hub_part,
        cut_part,
        weight_part,
    )
    back = over_chips(back)
    (row_sum,) = call(
        row_terms, [like((rows, feat), F32)], [SM] + [VM] * 4, 3 * unit, tile_cols, pack, weight_self, local_weight, gmean
    )
    (weight_sum,) = call(
        spread,
        [like((chips, share, feat))],
        [VM],
        1 << 20,
        back,
        to=[HB],
        scratch=[pltpu.VMEM((chips, share, feat), BF), DMA],
    )
    weight_all = over_chips(weight_sum)
    weight_pair = pair(weight_all)
    (feature_grad,) = call(
        finish,
        [like((rows, feat))],
        [SM] + [VM] * 4,
        2 * unit,
        row_counts,
        row_sum,
        routes,
        hub_ids,
        back,
    )
    grads = [like((feat, feat), F32)] * 2
    wide = [pltpu.VMEM((2, half, feat), F32), DMA((2,))]
    halfway = call(place_own, grads, [SM, VM], 1 << 20, core, weight_all, to=[HB, HB], scratch=wide)
    grad_self, grad_neigh = call(
        place_far,
        grads,
        [SM, VM, HB, HB],
        1 << 20,
        core,
        weight_pair,
        *halfway,
        to=[HB, HB],
        scratch=wide,
        alias={2: 0, 3: 1},
    )
    return activated, feature_grad, grad_self, grad_neigh


def solution(mesh):
    finer = Mesh(mesh.devices.reshape(4, 4, 4, 2), DOM)
    in_specs = (
        P(DOM, None),
        P(),
        P(),
        P(DOM, None),
        P(DOM, None),
        P(DOM, None),
        P(DOM, None),
        P(None, DOM),
        P(DOM),
        P(DOM, None),
        P(DOM, None),
        P(DOM),
        P(DOM, None),
    )
    out_specs = (P(DOM, None), P(DOM, None), P(), P())

    return jax.shard_map(
        per_device, mesh=finer, in_specs=in_specs, out_specs=out_specs, check_vma=False
    )
```

```python
import jax
import jax.numpy as jnp
from jax import lax
from jax.experimental import pallas as pl
from jax.experimental.pallas import tpu as pltpu
from jax.sharding import Mesh
from jax.sharding import PartitionSpec as P


TILE = 128
TPR = 4
DOM = ("dom_0", "dom_1", "dom_2", "dom_3")
CHIPS = DOM[:3]
CORE = "dom_3"
BF = jnp.bfloat16
F32 = jnp.float32
REACH = 256


VM = pl.BlockSpec(memory_space=pltpu.VMEM)
SM = pl.BlockSpec(memory_space=pltpu.SMEM)
HB = pl.BlockSpec(memory_space=pltpu.MemorySpace.HBM)
DMA = pltpu.SemaphoreType.DMA
LIMIT = 8 << 20


def call(body, outs, specs, flops, *args, scratch=(), to=None, alias=None, limit=LIMIT):
    size = sum(a.size * a.dtype.itemsize for a in args)
    size += sum(o.size * o.dtype.itemsize for o in outs)
    spaces = to or [VM] * len(outs)
    return pl.pallas_call(
        body,
        out_shape=tuple(
            pltpu.MemorySpace.HBM(o.shape, o.dtype) if p is HB else o for o, p in zip(outs, spaces)
        ),
        in_specs=list(specs),
        out_specs=tuple(spaces),
        scratch_shapes=list(scratch),
        input_output_aliases=alias or {},
        compiler_params=pltpu.CompilerParams(vmem_limit_bytes=limit),
        cost_estimate=pl.CostEstimate(flops=flops, bytes_accessed=size, transcendentals=0),
    )(*args)


def mm(a, b):
    return jnp.dot(a, b, preferred_element_type=F32)


def mm_nt(a, b):
    return lax.dot_general(a, b, (((1,), (1,)), ((), ())), preferred_element_type=F32)


def mm_tn(a, b):
    return lax.dot_general(a, b, (((0,), (0,)), ((), ())), preferred_element_type=F32)


def pair(x):
    return lax.ppermute(x, CORE, [(0, 1), (1, 0)])


def in_hbm(x):
    return pltpu.with_memory_space_constraint(x, pltpu.MemorySpace.HBM)


def over_chips(x):
    return lax.all_to_all(x, CHIPS, 0, 0, tiled=True)


def iota(shape, dim):
    return lax.broadcasted_iota(jnp.int32, shape, dim)


def ones_where(cond):
    return jnp.where(cond, 1.0, 0.0).astype(BF)


def small(ids):
    return ids.astype(F32).astype(BF)


def across(table, width):
    deep, peers = table.shape
    fan = ones_where(iota((peers, width), 0) == iota((peers, width), 1) // deep)
    wide = mm(small(table), fan)
    keep = iota((deep, width), 0) == iota((deep, width), 1) % deep
    return jnp.sum(jnp.where(keep, wide, 0.0), axis=0, keepdims=True)


def send(routes_at, hub_ids_at, feats_at, out, routes, hub_ids, feats, hubs_out, cuts_out, sem):
    reads = [
        pltpu.make_async_copy(routes_at, routes, sem.at[0]),
        pltpu.make_async_copy(hub_ids_at, hub_ids, sem.at[1]),
        pltpu.make_async_copy(feats_at.at[pl.ds(0, REACH)], feats, sem.at[2]),
    ]
    for read in reads:
        read.start()
    for read in reads:
        read.wait()
    deep, peers = routes.shape
    slots = deep * peers
    width = hub_ids.shape[1]
    same = iota((width, width), 0) == iota((width, width), 1)
    hub = jnp.sum(jnp.where(same, hub_ids[...].astype(F32), 0.0), axis=1, keepdims=True)
    slab = mm(ones_where(hub.astype(jnp.int32) == iota((width, REACH), 1)), feats[...])
    hubs_out[...] = jnp.broadcast_to(slab.astype(BF)[None], hubs_out.shape)
    first = pltpu.make_async_copy(hubs_out, out.at[:, pl.ds(0, width), :], sem.at[3])
    first.start()
    fan = ones_where(iota((slots, peers), 1) == iota((slots, peers), 0) // deep)
    wide = mm_nt(fan, small(routes[...]))
    keep = iota((slots, deep), 1) == iota((slots, deep), 0) % deep
    row = jnp.sum(jnp.where(keep, wide, 0.0), axis=1, keepdims=True).astype(jnp.int32)
    rows = mm(ones_where(row == iota((slots, REACH), 1)), feats[...])
    cuts_out[...] = rows.astype(BF).reshape(cuts_out.shape)
    second = pltpu.make_async_copy(
        cuts_out, out.at[:, pl.ds(width, cuts_out.shape[1]), :], sem.at[4]
    )
    second.start()
    first.wait()
    second.wait()


def ahead(
    cols,
    count,
    core,
    feats_at,
    lweight_at,
    cweight_at,
    wself_at,
    counts,
    edges,
    hubw,
    local_sum_at,
    self_term_at,
    dense_at,
    flip_own_at,
    cut_own_at,
    wide_own_at,
    feat_own_at,
    dense_far_at,
    wide_far_at,
    degree_at,
    ship,
    feats,
    lweight,
    cweight,
    wself,
    local_sum,
    self_term,
    dense,
    flip_own,
    cut_own,
    wide_own,
    feat_own,
    dense_far,
    wide_far,
    degree,
    masked,
    picked,
    sem,
):
    reads = [
        pltpu.make_async_copy(src, dst, sem.at[i])
        for i, (src, dst) in enumerate(
            ((cweight_at, cweight), (feats_at, feats), (lweight_at, lweight), (wself_at, wself))
        )
    ]
    for read in reads:
        read.start()
    writes = []

    def put(src, dst):
        write = pltpu.make_async_copy(src, dst, sem.at[4 + len(writes)])
        write.start()
        writes.append(write)

    rows, feat = feats.shape
    slots = cweight.shape[1]
    hubs = 2 * flip_own.shape[0]
    blocks = rows // TILE
    live = count[0]
    me = core[0]
    edge_w = hubw[...]
    deep = slots // counts.shape[1]
    width = hubs // (2 * (slots // (2 * deep)))
    owner = edges[...] // width
    place = ((owner % 2) ^ me) * (hubs // 2) + (owner // 2) * width + edges[...] % width
    weight = edge_w.astype(F32)
    step = 128

    def build(i, carry):
        base = pl.multiple_of(i * step, step)
        hub = iota((step, rows), 0) + base
        acc = jnp.zeros((step, rows), F32)
        for k in range(edges.shape[0]):
            acc = acc + jnp.where(place[k : k + 1, :] == hub, weight[k : k + 1, :], 0.0)
        flat = acc.astype(BF)

        @pl.when(base < hubs // 2)
        def _():
            flip_own[pl.ds(base, step), :] = flat
            dense[:, pl.ds(base, step)] = jnp.transpose(flat)

        @pl.when(base >= hubs // 2)
        def _():
            spot = pl.multiple_of(base - hubs // 2, step)
            ship[pl.ds(spot, step), :] = flat
            dense_far[:, pl.ds(spot, step)] = jnp.transpose(flat)

        return carry

    lax.fori_loop(0, hubs // step, build, 0)
    put(flip_own, flip_own_at)
    put(dense, dense_at)
    put(dense_far, dense_far_at)
    fan = ones_where(iota((counts.shape[1], slots), 0) == iota((counts.shape[1], slots), 1) // deep)
    used = mm(small(counts[...]), fan)
    on = (iota((1, slots), 1) % deep).astype(F32) < used
    reads[0].wait()
    cut = cweight[...] * jnp.broadcast_to(ones_where(on), (rows, slots))
    hub_deg = mm_tn(edge_w, jnp.ones((edge_w.shape[0], TILE), BF))[:, :1]
    degree[...] = hub_deg + jnp.sum(cut.astype(F32), axis=1, keepdims=True)
    flip = jnp.transpose(cut)
    side = (iota((slots, rows), 0) // deep) % 2
    kept = jnp.where(side == me, flip, jnp.zeros_like(flip))
    tall = flip.astype(F32)
    up = pltpu.roll(tall, slots - deep, 0)
    down = pltpu.roll(tall, deep, 0)
    moved = jnp.where(side == me, jnp.where(me == 0, up, down), 0.0).astype(BF)
    cut_own[...] = kept
    put(cut_own, cut_own_at)
    wide_own[...] = jnp.transpose(kept)
    put(wide_own, wide_own_at)
    ship[hubs // 2 : hubs // 2 + slots, :] = moved
    wide_far[...] = jnp.transpose(moved)
    put(wide_far, wide_far_at)
    reads[1].wait()
    half = feat // 2
    feat_own[...] = jnp.transpose(jnp.where(me == 0, feats[:, :half], feats[:, half:]))
    put(feat_own, feat_own_at)
    ship[hubs // 2 + slots :, :] = jnp.transpose(
        jnp.where(me == 0, feats[:, half:], feats[:, :half])
    )
    masked[...] = jnp.where(iota((rows, feat), 0) < live, feats[...], jnp.zeros_like(feats))
    reads[2].wait()
    lane = iota((TILE, TILE), 1)
    for r in range(blocks):
        part = jnp.zeros((TILE, 1), F32)
        at = pl.ds(r * TILE, TILE)
        for t in range(TPR):
            base = cols[r, t] * TILE
            picked[pl.ds(t * TILE, TILE), :] = masked[pl.ds(pl.multiple_of(base, TILE), TILE), :]
            vals = lweight[at, pl.ds(t * TILE, TILE)].astype(F32)
            part = part + jnp.sum(jnp.where(lane + base < live, vals, 0.0), axis=1, keepdims=True)
        local_sum[at, :] = mm(lweight[at, :], picked[...])
        degree[at, :] += part
    put(local_sum, local_sum_at)
    put(degree, degree_at)
    reads[3].wait()
    self_term[...] = mm(masked[...], wself[...])
    put(self_term, self_term_at)
    for write in writes:
        write.wait()


def sides(bundle, width, feat):
    peers, deep, _ = bundle.shape
    table = bundle[:, :width, :].reshape(peers * width, feat)
    return table, bundle[:, width:, :].reshape(peers * (deep - width), feat)


def settle(ship_in, degree_in, ship, degree):
    pass


def near_sum(
    wide_at,
    dense_at,
    local_at,
    dense_far_at,
    wide_far_at,
    self_at,
    degree_at,
    cot_at,
    wneigh_at,
    bundle,
    out,
    dense_far,
    wide_far,
    self_term,
    degree,
    cot,
    wneigh,
    wide,
    dense,
    local,
    sem,
):
    pairs = (
        (wide_at, wide),
        (dense_at, dense),
        (local_at, local),
        (wide_far_at, wide_far),
        (dense_far_at, dense_far),
        (self_at, self_term),
        (degree_at, degree),
        (wneigh_at, wneigh),
        (cot_at, cot),
    )
    reads = [pltpu.make_async_copy(src, dst, sem.at[i]) for i, (src, dst) in enumerate(pairs)]
    for read in reads:
        read.start()
    _, feat = out.shape
    table, cut = sides(bundle, dense.shape[1] // bundle.shape[0], feat)
    reads[0].wait()
    total = mm(wide[...], cut)
    reads[1].wait()
    total = total + mm(dense[...], table)
    reads[2].wait()
    out[...] = total + local[...]
    for read in reads[3:]:
        read.wait()


def forward(
    core,
    count,
    flip_at,
    cut_at,
    feat_at,
    ship_at,
    degree_far_at,
    near,
    wide_far,
    dense,
    bundle,
    degree,
    self_term,
    wneigh,
    cot,
    act_at,
    mean_own,
    pack,
    flip,
    cut_own,
    feat_own,
    ship,
    degree_far,
    act,
    sem,
):
    pairs = (
        (flip_at, flip),
        (cut_at, cut_own),
        (feat_at, feat_own),
        (ship_at, ship),
        (degree_far_at, degree_far),
    )
    reads = [pltpu.make_async_copy(src, dst, sem.at[i]) for i, (src, dst) in enumerate(pairs)]
    for read in reads:
        read.start()
    rows, feat = near.shape
    half = feat // 2
    me = core[0] % 2
    table, cut = sides(bundle, dense.shape[1] // bundle.shape[0], feat)
    step = rows // 4
    for i in range(4):
        at = pl.ds(i * step, step)
        total = near[at, :] + mm(wide_far[at, :], cut) + mm(dense[at, :], table)
        mean = (total / degree[at, :]).astype(BF)
        mean_own[:, at] = jnp.transpose(jnp.where(me == 0, mean[:, :half], mean[:, half:]))
        pack[:half, at] = jnp.transpose(jnp.where(me == 0, mean[:, half:], mean[:, :half]))
        live = iota((step, feat), 0) + i * step < count[0]
        pre = self_term[at, :] + mm(mean, wneigh[...])
        sig = jax.nn.sigmoid(pre)
        act[at, :] = jnp.where(live, pre * sig, 0.0).astype(BF)
        reads.append(pltpu.make_async_copy(act.at[at], act_at.at[at], sem.at[len(reads)]))
        reads[-1].start()
        grad = cot[at, :].astype(F32) * sig * (1.0 + pre * (1.0 - sig))
        pack[pl.ds(half + i * step, step), :] = jnp.where(live, grad, 0.0).astype(BF)
    for read in reads:
        read.wait()


def back_near(pack, wneigh, degree, flip_own, cut_own, gmean, hub, cut, near, sem):
    half = wneigh.shape[0] // 2
    near[...] = (mm_nt(pack[half:, :], wneigh[...]) / degree[...]).astype(BF)
    away = pltpu.make_async_copy(near, gmean, sem)
    away.start()
    hub[...] = mm(flip_own[...], near[...])
    cut[...] = mm(cut_own[...], near[...])
    away.wait()


def weight_near(pack, mean_own, feat_own, out):
    half = feat_own.shape[0]
    grad = pack[half:, :]
    out[:half, :] = mm(feat_own[...], grad)
    out[half:, :] = mm(mean_own[...], grad)


def back_far(pack, wneigh, degree, ship, hub, cut, weight, out):
    feat = wneigh.shape[0]
    half = feat // 2
    hubs, slots = hub.shape[0], cut.shape[0]
    peers = out.shape[0]
    width, deep = hubs // peers, (hubs + slots) // peers
    share = out.shape[1] - deep
    grad = pack[half:, :]
    far = (mm_nt(grad, wneigh[...]) / degree[...]).astype(BF)
    low = weight[:half, :] + mm(ship[hubs + slots :, :], grad)
    out[: peers // 2, deep:, :] = low.astype(BF).reshape(peers // 2, share, feat)
    high = weight[half:, :] + mm(pack[:half, :], grad)
    out[peers // 2 :, deep:, :] = high.astype(BF).reshape(peers // 2, share, feat)
    first = hub[...] + mm(ship[:hubs, :], far)
    out[:, :width, :] = first.astype(BF).reshape(peers, width, feat)
    second = cut[...] + mm(ship[hubs : hubs + slots, :], far)
    out[:, width:deep, :] = second.astype(BF).reshape(peers, deep - width, feat)


def row_terms(cols, pack, wself, lweight, gmean, out):
    rows, feat = out.shape
    out[...] = mm_nt(pack[feat // 2 :, :], wself[...])
    for r in range(rows // TILE):
        at = pl.ds(r * TILE, TILE)
        part = mm_tn(lweight[at, :], gmean[at, :])
        for t in range(TPR):
            base = pl.multiple_of(cols[r, t] * TILE, TILE)
            out[pl.ds(base, TILE), :] += part[t * TILE : (t + 1) * TILE, :]


def spread(parts, out, held, sem):
    share = held.shape[1]
    first = parts.shape[1] - share
    total = jnp.sum(parts[:, first:, :].astype(F32), axis=0)
    held[...] = jnp.broadcast_to(total.astype(BF)[None], held.shape)
    away = pltpu.make_async_copy(held, out, sem)
    away.start()
    away.wait()


def finish(count, rows_in, routes, hub_ids, bundle, out):
    rows, feat = rows_in.shape
    deep, peers = routes.shape
    slots = deep * peers
    chips = bundle.shape[0]
    width = hub_ids.shape[1]
    hubs = chips * width
    ids = across(routes[...], slots).astype(jnp.int32)
    cut = bundle[:, width : width + slots // chips, :].reshape(slots, feat)
    top = mm(ones_where(ids == iota((REACH, slots), 0)), cut)
    fan = ones_where(iota((width, hubs), 0) == iota((width, hubs), 1) % width)
    spots = mm(small(hub_ids[...]), fan).astype(jnp.int32)
    table = bundle[:, :width, :].reshape(hubs, feat)
    top = top + mm(ones_where(spots == iota((REACH, hubs), 0)), table)
    live = iota((rows, feat), 0) < count[0]
    out[:REACH, :] = jnp.where(live[:REACH], rows_in[:REACH, :] + top, 0.0).astype(BF)
    out[REACH:, :] = jnp.where(live[REACH:], rows_in[REACH:, :], 0.0).astype(BF)


def place_rows(turn, source, first, second, held, sem):
    half, feat = held.shape[1:]
    whole = source[...].reshape(2 * half, feat).astype(F32)
    at = pl.ds(pl.multiple_of(turn * half, half), half)
    held[0] = whole[:half, :]
    one = pltpu.make_async_copy(held.at[0], first.at[at], sem.at[0])
    one.start()
    held[1] = whole[half:, :]
    two = pltpu.make_async_copy(held.at[1], second.at[at], sem.at[1])
    two.start()
    one.wait()
    two.wait()


def place_own(core, source, first, second, held, sem):
    place_rows(core[0], source, first, second, held, sem)


def place_far(core, source, first_in, second_in, first, second, held, sem):
    place_rows(1 - core[0], source, first, second, held, sem)


def per_device(
    features,
    weight_self,
    weight_neigh,
    local_weight,
    tile_cols,
    cut_weight,
    send_rows,
    send_count,
    hub_rows,
    hub_edges,
    hub_weight,
    row_counts,
    cotangent,
):
    rows, feat = features.shape
    core = lax.axis_index(CORE).astype(jnp.int32).reshape(1)
    chips = lax.axis_size(CHIPS)
    deep = send_rows.shape[1]
    width = hub_rows.shape[0]
    hubs = chips * 2 * width
    slots = chips * 2 * deep
    half = feat // 2
    share = feat // chips
    unit = 2 * 512 * 512 * 512

    def like(shape, kind=BF):
        return jax.ShapeDtypeStruct(shape, kind)

    routes = send_rows.T
    hub_ids = hub_rows.reshape(1, width)
    (bundle,) = call(
        send,
        [like((chips, width + 2 * deep, feat))],
        [HB] * 3,
        unit,
        *[in_hbm(x) for x in (routes, hub_ids, features)],
        to=[HB],
        scratch=[
            pltpu.VMEM(routes.shape, routes.dtype),
            pltpu.VMEM(hub_ids.shape, hub_ids.dtype),
            pltpu.VMEM((REACH, feat), BF),
            pltpu.VMEM((chips, width, feat), BF),
            pltpu.VMEM((chips, 2 * deep, feat), BF),
            DMA((5,)),
        ],
    )
    bundle = over_chips(bundle)
    held = [
        like((rows, feat), F32),
        like((rows, feat), F32),
        like((rows, hubs // 2)),
        like((hubs // 2, rows)),
        like((slots, rows)),
        like((rows, slots)),
        like((half, rows)),
        like((rows, hubs // 2)),
        like((rows, slots)),
        like((rows, 1), F32),
    ]
    sources = (features, local_weight, cut_weight, weight_self)
    (
        local_sum,
        self_term,
        dense,
        flip_own,
        cut_own,
        wide_own,
        feat_own,
        dense_far,
        wide_far,
        degree,
        ship,
    ) = call(
        ahead,
        held + [like((hubs // 2 + slots + half, rows))],
        [SM, SM, SM] + [HB] * 4 + [VM] * 3,
        40 * unit,
        tile_cols,
        row_counts,
        core,
        *[in_hbm(x) for x in sources],
        send_count.T,
        hub_edges.T,
        hub_weight.T,
        to=[HB] * len(held) + [VM],
        scratch=[pltpu.VMEM(x.shape, x.dtype) for x in (*sources, *held)]
        + [pltpu.VMEM((rows, feat), BF), pltpu.VMEM((TPR * TILE, feat), BF), DMA((4 + len(held),))],
        limit=20 << 20,
    )
    ship_far, degree_far = call(
        settle,
        [like(ship.shape), like(degree.shape, F32)],
        [HB] * 2,
        1 << 20,
        in_hbm(pair(ship)),
        in_hbm(pair(degree)),
        to=[HB] * 2,
        alias={0: 0, 1: 1},
    )
    bundle_far = pair(bundle)
    following = [dense_far, wide_far, self_term, degree, cotangent, weight_neigh]
    near, dense_far, wide_far, self_term, degree, cotangent, weight_neigh = call(
        near_sum,
        [like((rows, feat), F32)] + [like(x.shape, x.dtype) for x in following],
        [HB] * 9 + [VM],
        3 * unit,
        *[in_hbm(x) for x in (wide_own, dense, local_sum, *following)],
        bundle,
        scratch=[pltpu.VMEM(x.shape, x.dtype) for x in (wide_own, dense, local_sum)] + [DMA((9,))],
    )
    following = [flip_own, cut_own, feat_own, ship_far, degree_far]
    activated, mean_own, pack, flip_own, cut_own, feat_own, ship_far, degree_far = call(
        forward,
        [like((rows, feat)), like((half, rows)), like((half + rows, feat))]
        + [like(x.shape, x.dtype) for x in following],
        [SM, SM] + [HB] * 5 + [VM] * 8,
        4 * unit,
        core,
        row_counts,
        *[in_hbm(x) for x in following],
        near,
        wide_far,
        dense_far,
        bundle_far,
        degree,
        self_term,
        weight_neigh,
        cotangent,
        to=[HB] + [VM] * 7,
        scratch=[pltpu.VMEM((rows, feat), BF), DMA((9,))],
    )
    pack_far = pair(pack)
    gmean, hub_part, cut_part = call(
        back_near,
        [like((rows, feat)), like((hubs // 2, feat), F32), like((slots, feat), F32)],
        [VM] * 5,
        4 * unit,
        pack,
        weight_neigh,
        degree,
        flip_own,
        cut_own,
        to=[HB, VM, VM],
        scratch=[pltpu.VMEM((rows, feat), BF), DMA],
    )
    (weight_part,) = call(weight_near, [like((feat, feat), F32)], [VM] * 3, unit, pack, mean_own, feat_own)
    (back,) = call(
        back_far,
        [like((chips, width + 2 * deep + share, feat))],
        [VM] * 7,
        5 * unit,
        pack_far,
        weight_neigh,
        degree_far,
        ship_far,
        hub_part,
        cut_part,
        weight_part,
    )
    back = over_chips(back)
    (row_sum,) = call(
        row_terms, [like((rows, feat), F32)], [SM] + [VM] * 4, 3 * unit, tile_cols, pack, weight_self, local_weight, gmean
    )
    (weight_sum,) = call(
        spread,
        [like((chips, share, feat))],
        [VM],
        1 << 20,
        back,
        to=[HB],
        scratch=[pltpu.VMEM((chips, share, feat), BF), DMA],
    )
    weight_all = over_chips(weight_sum)
    weight_pair = pair(weight_all)
    (feature_grad,) = call(
        finish,
        [like((rows, feat))],
        [SM] + [VM] * 4,
        2 * unit,
        row_counts,
        row_sum,
        routes,
        hub_ids,
        back,
    )
    grads = [like((feat, feat), F32)] * 2
    wide = [pltpu.VMEM((2, half, feat), F32), DMA((2,))]
    halfway = call(place_own, grads, [SM, VM], 1 << 20, core, weight_all, to=[HB, HB], scratch=wide)
    grad_self, grad_neigh = call(
        place_far,
        grads,
        [SM, VM, HB, HB],
        1 << 20,
        core,
        weight_pair,
        *halfway,
        to=[HB, HB],
        scratch=wide,
        alias={2: 0, 3: 1},
    )
    return activated, feature_grad, grad_self, grad_neigh


def solution(mesh):
    finer = Mesh(mesh.devices.reshape(4, 4, 4, 2), DOM)
    in_specs = (
        P(DOM, None),
        P(),
        P(),
        P(DOM, None),
        P(DOM, None),
        P(DOM, None),
        P(DOM, None),
        P(None, DOM),
        P(DOM),
        P(DOM, None),
        P(DOM, None),
        P(DOM),
        P(DOM, None),
    )
    out_specs = (P(DOM, None), P(DOM, None), P(), P())

    return jax.shard_map(
        per_device, mesh=finer, in_specs=in_specs, out_specs=out_specs, check_vma=False
    )
```
